32 devices in a mesh: groups: 2 (over x), dp: 16 (over z, y, core).
Axes of the slice: x: 2, y: 2, z: 4, core: 2. Of those that a mesh axis runs over, the one named last changes fastest.
Arguments:
- wave: float32 [2048, 320], P(('groups', 'dp')), parts along dimension 0, may hold values from -7.5 to 7.5
- row_slot: int32 [2048], P(('groups', 'dp')), parts along dimension 0, may hold values from 0 to 1023, as said below
- frame_lengths: int32 [128], P('groups'), parts along dimension 0, may hold values from 1 to 256, 1024 in all
- sample_trim: int32 [128], P('groups'), parts along dimension 0, may hold values from 0 to 319
- first_weight: float32 [10, 512], replicated, may hold values from -2 to 2
- mid_weight: bfloat16 [4, 3, 512, 512], replicated, may hold values from -0.15625 to 0.15625
- tail_weight: bfloat16 [2, 2, 512, 512], replicated, may hold values from -0.1875 to 0.1875
Outputs:
- centered: bfloat16 [2048, 512], P(('groups', 'dp')), parts along dimension 0
The draws below stay inside these ranges and needn't reach their ends.
There are 2 independent parts, one for each index of `groups`. The reference program is written for one: setup_inputs(seed, part) draws one part's arguments, and reference() takes and returns one part's arrays. A program takes and returns all parts, laid end to end along the dimension named above; an argument that names none is the same for every part. Nothing has to cross between parts.
Inputs may be any that keep to these rules, and one draw needn't show every extreme that they name: row_slot is a permutation of 0 .. 1023. For every index h of dp and every index o, at most 6 of the 64 rows of h have row_slot in [o * 64, (o + 1) * 64), and for every h exactly one o receives 6 of them. frame_lengths sum to 1024, and the largest is 256.
All inputs are finite; a program needn't handle non-finite values.
Results may differ from the reference program's by a relative error of at most 0.023.
Values sent between devices are 32-bit elements; how exact they have to be, the bound alone decides.
A program may use at most 64 MiB of HBM per device.

```python
import math
import jax
import jax.numpy as jnp
import numpy as np
from jax import lax

C1 = 512
BLOCK = 320
LOOK = 80
MID = 4
TAIL = 2
F_DEV = 64
FRAMES = 1024
ROLLS = 64
MAXLEN = 256
CAP = 6


def make_slots(key):
    owners = FRAMES // F_DEV
    keys_all = jax.random.split(jax.random.fold_in(key, 11), 5)
    ranking = jax.random.permutation(keys_all[0], owners)
    leftover_rows = F_DEV - CAP
    baseline = leftover_rows // (owners - 1)
    leftover = leftover_rows % (owners - 1)
    position = jnp.arange(owners, dtype=jnp.int32)
    sorted_load = jnp.where(position == 0, CAP, baseline + (position - 1 < leftover).astype(jnp.int32))
    multiplicity = jnp.zeros((owners,), jnp.int32).at[ranking].set(sorted_load)
    owner_perm = jax.random.permutation(keys_all[1], owners)
    holder_perm = jax.random.permutation(keys_all[2], owners)
    counts = multiplicity[(owner_perm[None, :] - holder_perm[:, None]) % owners]
    cumulative = jnp.cumsum(counts, axis=0)
    within = jnp.arange(F_DEV, dtype=jnp.int32)
    sources = jnp.sum((cumulative.T[:, None, :] <= within[None, :, None]).astype(jnp.int32), axis=2)
    shuffles = jax.vmap(lambda single_key: jax.random.permutation(single_key, F_DEV))(jax.random.split(keys_all[3], owners))
    shuffled = jnp.take_along_axis(sources, shuffles, axis=1).reshape(-1)
    scores = shuffled * FRAMES + jax.random.permutation(keys_all[4], FRAMES)
    return jnp.argsort(scores, stable=True).astype(jnp.int32)


def draw_row_slot(key, part):
    return make_slots(key)


def draw_wave(key, part):
    slots = make_slots(key)
    region_frames = F_DEV // 2
    regions = FRAMES // region_frames
    keys_all = jax.random.split(jax.random.fold_in(key, 23), 6)
    offset = jax.random.uniform(keys_all[0], (regions,), jnp.float32, -1.5, 1.5)
    strength = jax.random.uniform(keys_all[1], (regions,), jnp.float32, 0.0, 1.5)
    omega = jnp.exp(jax.random.uniform(keys_all[2], (regions,), jnp.float32, math.log(0.02), math.log(0.6)))
    phase = jax.random.uniform(keys_all[3], (regions,), jnp.float32, -math.pi, math.pi)
    loudness = jnp.exp(jax.random.uniform(keys_all[4], (regions,), jnp.float32, math.log(0.25), math.log(1.5)))
    noise = jnp.clip(jax.random.normal(keys_all[5], (FRAMES, BLOCK), jnp.float32), -3.0, 3.0)
    region_of = slots // region_frames
    sample_pos = jnp.arange(BLOCK, dtype=jnp.float32)[None, :]
    tone = strength[region_of][:, None] * jnp.sin(omega[region_of][:, None] * sample_pos + phase[region_of][:, None])
    return offset[region_of][:, None] + loudness[region_of][:, None] * noise + tone


def with_ends(entries, key, smallest, top_value):
    dims = entries.shape
    place = [jax.random.randint(jax.random.fold_in(key, axis), (), 0, dims[axis]) for axis in range(len(dims))]
    entries = entries.at[tuple(place)].set(smallest)
    longest = dims.index(max(dims))
    place[longest] = (place[longest] + 1) % dims[longest]
    return entries.at[tuple(place)].set(top_value)


def length_profile(count, total, reach, skew):
    portions = [(1 << 20) // math.isqrt(standing ** skew) + 1 for standing in range(2, count + 1)]
    spare, given = total - reach - (count - 1), [1] * (count - 1)
    while spare > 0:
        movable = [i for i in range(count - 1) if given[i] < reach]
        mass, left = sum([portions[i] for i in movable]), spare
        for i in movable:
            addition = min(reach - given[i], max(1, left * portions[i] // mass), spare)
            given[i] = given[i] + addition
            spare = spare - addition
    return np.array([reach] + given)


def ragged_sizes(rng, count, total, reach, skew):
    if count == 2:
        one = jax.random.randint(rng, (), max(1, total - reach), min(reach, total - 1) + 1)
        return jnp.stack([one, total - one])
    lengths = jnp.asarray(length_profile(count, total, reach, skew), jnp.int32)
    pairs = (count - 1) // 2
    donor, receiver = lengths[1:1 + 2 * pairs:2], lengths[2:2 + 2 * pairs:2]
    margin = jnp.minimum(donor - 1, reach - receiver)
    moved = jax.random.randint(jax.random.fold_in(rng, 1), (pairs,), 0, 1 << 20) % (margin + 1)
    lengths = lengths.at[1:1 + 2 * pairs:2].set(donor - moved).at[2:2 + 2 * pairs:2].set(receiver + moved)
    return lengths[jax.random.permutation(jax.random.fold_in(rng, 2), count)]


def scatter_about(own_key, dims, width, most, kind=jnp.bfloat16):
    array = width * jax.random.normal(own_key, dims, jnp.float32)
    return jnp.clip(array, min=-most, max=most).astype(kind)


def setup_inputs(seed: int = 0, part: int = 0) -> dict:
    splits = jax.random.split(jax.random.key(seed), 8)
    part_splits = jax.random.split(jax.random.fold_in(splits[7], part), 8)
    wave = draw_wave(jax.random.fold_in(jax.random.fold_in(splits[7], part), 71), part)
    row_slot = draw_row_slot(jax.random.fold_in(jax.random.fold_in(splits[7], part), 71), part)
    frame_lengths = ragged_sizes(part_splits[2], ROLLS, FRAMES, MAXLEN, 2).astype(jnp.int32)
    sample_trim = with_ends(jax.random.randint(part_splits[3], (ROLLS,), 0, BLOCK), jax.random.fold_in(part_splits[3], 1), 0, BLOCK - 1).astype(jnp.int32)
    first_weight = scatter_about(splits[4], (10, C1), 10 ** -0.5, 2.0, jnp.float32)
    mid_weight = scatter_about(splits[5], (MID, 3, C1, C1), (3 * C1) ** -0.5, 0.15625)
    tail_weight = scatter_about(splits[6], (TAIL, 2, C1, C1), (2 * C1) ** -0.5, 0.1875)
    return {"wave": wave, "row_slot": row_slot, "frame_lengths": frame_lengths, "sample_trim": sample_trim, "first_weight": first_weight, "mid_weight": mid_weight, "tail_weight": tail_weight}


def norm_gelu(values):
    average = lax.optimization_barrier(jnp.mean(values, axis=-1, keepdims=True))
    centred = values - average
    spread = lax.optimization_barrier(jnp.mean(centred * centred, axis=-1, keepdims=True))
    return jax.nn.gelu(centred / jnp.sqrt(spread + 1e-05), approximate=False).astype(jnp.bfloat16)

def strided(inputs, weight, stride):
    kernel = weight.shape[0]
    length = (inputs.shape[0] - kernel) // stride + 1
    summed = jnp.zeros((length, weight.shape[2]), jnp.float32)
    for offset in range(kernel):
        shifted = lax.slice_in_dim(inputs, offset, offset + stride * (length - 1) + 1, stride, 0)
        summed = summed + jnp.dot(shifted, weight[offset], preferred_element_type=jnp.float32)
    return summed

def frontend(samples, first_weight, mid_weight, tail_weight):
    fifths = samples.reshape(-1, 5)
    patches = jnp.concatenate([fifths[:-1], fifths[1:]], axis=1)
    hidden = norm_gelu(jnp.dot(patches, first_weight, precision=lax.Precision.HIGHEST, preferred_element_type=jnp.float32))
    for step_index in range(MID):
        hidden = norm_gelu(strided(hidden, mid_weight[step_index], 2))
    for step_index in range(TAIL):
        hidden = norm_gelu(strided(hidden, tail_weight[step_index], 2))
    return hidden

def reference(wave, row_slot, frame_lengths, sample_trim, first_weight, mid_weight, tail_weight):
    stream = jnp.zeros((FRAMES, BLOCK), jnp.float32).at[row_slot].set(wave)
    starts = jnp.cumsum(frame_lengths) - frame_lengths
    frame_ids = jnp.arange(FRAMES, dtype=jnp.int32)
    rollout = lax.optimization_barrier(jnp.sum((starts[None, :] <= frame_ids[:, None]).astype(jnp.int32), axis=1)) - 1
    sample_limit = BLOCK * frame_lengths - sample_trim
    within = ((frame_ids - starts[rollout]) * BLOCK)[:, None] + jnp.arange(BLOCK, dtype=jnp.int32)[None, :]
    signal = jnp.where(within < sample_limit[rollout][:, None], stream, 0.0)
    padded = jnp.concatenate([signal.reshape(-1), jnp.zeros((LOOK,), jnp.float32)])

    def one_block(block_index):
        begin = (block_index * (F_DEV * BLOCK)).astype(jnp.int32)
        samples = lax.dynamic_slice_in_dim(padded, begin, F_DEV * BLOCK + LOOK)
        return frontend(samples, first_weight, mid_weight, tail_weight)
    blocks = FRAMES // F_DEV
    features = lax.map(one_block, jnp.arange(blocks, dtype=jnp.int32)).reshape(FRAMES, -1)
    rollout_sum = jax.ops.segment_sum(features.astype(jnp.float32), rollout, num_segments=ROLLS)
    rollout_mean = rollout_sum / frame_lengths[:, None].astype(jnp.float32)
    return (features.astype(jnp.float32) - rollout_mean[rollout]).astype(jnp.bfloat16)
```

```python
import functools

import jax
import jax.numpy as jnp
from jax import lax
from jax.experimental import pallas as pl
from jax.experimental.pallas import tpu as pltpu
from jax.sharding import PartitionSpec as P

BLOCK = 320
LOOK = 80
LANES = 128
MAXLEN = 256
EPS = 1e-05
HALF_ROOT = 0.7071067811865476
F32 = jnp.float32
BF16 = jnp.bfloat16


def iota(shape, dim):
    return lax.broadcasted_iota(jnp.int32, shape, dim).astype(F32)


def to_column(row):
    size = row.shape[1]
    same = iota((size, size), 0) == iota((size, size), 1)
    return jnp.sum(jnp.where(same, row, 0.0), axis=1, keepdims=True)


def to_row(column):
    size = column.shape[0]
    same = iota((size, size), 0) == iota((size, size), 1)
    return jnp.sum(jnp.where(same, column, 0.0), axis=0, keepdims=True)


def two_parts(values):
    high = values.astype(BF16)
    return high, (values - high.astype(F32)).astype(BF16)


def unit_gelu(centred, eps):
    spread = jnp.mean(centred * centred, axis=-1, keepdims=True)
    scaled = centred * (lax.rsqrt(spread + eps) * HALF_ROOT)
    return scaled + scaled * lax.erf(scaled)


def norm_unit_gelu(values, eps):
    return unit_gelu(values - jnp.mean(values, axis=-1, keepdims=True), eps)


class Packing:
    def __init__(self, cap):
        self.cap = cap
        self.pairs = (cap + 1) // 2
        self.meta = 2 * cap + self.pairs
        self.stride = (self.meta + 1 + 7) // 8 * 8


def pack(n, packing, wave_ref, slot_ref, send):
    rows = wave_ref.shape[0]
    cap, stride = packing.cap, packing.stride
    slot_row = slot_ref[...].astype(F32)
    slot_col = to_column(slot_row)
    target_row = jnp.floor(slot_row / rows)
    target_col = jnp.floor(slot_col / rows)
    alike = target_col == target_row
    earlier = iota((rows, rows), 0) < iota((rows, rows), 1)
    later = iota((rows, rows), 0) > iota((rows, rows), 1)
    rank_row = jnp.sum(jnp.where(earlier & alike, 1.0, 0.0), axis=0, keepdims=True)
    rank_col = jnp.sum(jnp.where(later & alike, 1.0, 0.0), axis=1, keepdims=True)
    base = target_row * stride
    half_rank = jnp.floor(rank_row / 2.0)
    odd = rank_row - 2.0 * half_rank == 1.0
    pair = base + 2 * cap + half_rank
    ahead = jnp.where(target_row * rows == slot_row, base - stride + packing.meta, -1.0)
    places = [
        base + rank_row,
        base + cap + rank_row,
        jnp.where(odd, -1.0, pair),
        jnp.where(odd, pair, -1.0),
        ahead,
        base + packing.meta,
    ]
    place = iota((n * stride, rows), 0)
    pick = jnp.concatenate([jnp.where(place == p, 1.0, 0.0) for p in places], axis=1).astype(BF16)
    lane = iota((rows, LANES), 1)
    tile0 = wave_ref[:, :LANES]
    tile1 = wave_ref[:, LANES : 2 * LANES]
    rest = jnp.concatenate([wave_ref[:, 2 * LANES : BLOCK], jnp.zeros((rows, 3 * LANES - BLOCK), F32)], axis=1)
    blocks = [
        tile0,
        tile1,
        rest,
        pltpu.roll(rest, LANES // 2, 1),
        jnp.where(lane < LOOK, tile0, 0.0),
        jnp.where(lane == LOOK + rank_col, slot_col + 1.0, 0.0),
    ]
    high, low = two_parts(jnp.concatenate(blocks, axis=0))
    send[...] = jnp.dot(pick, high, preferred_element_type=F32) + jnp.dot(pick, low, preferred_element_type=F32)


def greet(n):
    me = lax.axis_index("dp")

    def one(k, carry):
        pl.semaphore_signal(
            pltpu.get_barrier_semaphore(), inc=1, device_id={"dp": lax.rem(me + k, n)}
        )
        return carry

    lax.fori_loop(1, n, one, 0)


def scatter(n, stride, send, recv, send_sem, recv_sem):
    me = lax.axis_index("dp")
    mine = pl.ds(pl.multiple_of(me * stride, stride), stride)
    recv[mine, :] = send[mine, :]
    pl.semaphore_wait(pltpu.get_barrier_semaphore(), n - 1)
    upper = me // (n // 2)

    def begin(k, carry):
        to = upper * k + (1 - upper) * (n - 1 - k)

        @pl.when(to != me)
        def _():
            pltpu.make_async_remote_copy(
                src_ref=send.at[pl.ds(pl.multiple_of(to * stride, stride), stride)],
                dst_ref=recv.at[mine],
                send_sem=send_sem.at[to],
                recv_sem=recv_sem.at[me],
                device_id={"dp": to},
            ).start()

        return carry

    lax.fori_loop(0, n, begin, 0)


def gather(n, stride, send, recv, send_sem, recv_sem):
    me = lax.axis_index("dp")
    mine = pl.ds(pl.multiple_of(me * stride, stride), stride)

    def finish(k, carry):
        other = lax.rem(me + k, n)
        theirs = pl.ds(pl.multiple_of(other * stride, stride), stride)
        copy = pltpu.make_async_remote_copy(
            src_ref=send.at[mine],
            dst_ref=recv.at[theirs],
            send_sem=send_sem.at[other],
            recv_sem=recv_sem.at[other],
            device_id={"dp": other},
        )
        copy.wait_recv()
        copy.wait_send()
        return carry

    lax.fori_loop(1, n, finish, 0)


def spans(frames, rows, length_ref):
    first = lax.axis_index("dp").astype(F32) * rows
    length_row = length_ref[...].astype(F32)
    count = length_row.shape[1]
    length_col = to_column(length_row)
    before = iota((count, count), 0) < iota((count, count), 1)
    start_row = jnp.sum(jnp.where(before, length_col, 0.0), axis=0, keepdims=True)
    end_row = start_row + length_row
    frame = iota((frames, count), 0) + first
    member = (start_row <= frame) & (frame < end_row)
    start = jnp.sum(jnp.where(member, start_row, 0.0), axis=1, keepdims=True)
    end = jnp.sum(jnp.where(member, end_row, 0.0), axis=1, keepdims=True)
    return member, frame, start, end, end_row


def keep_limit(frames, rows, length_ref, trim_ref, limit):
    member, frame, _, _, end_row = spans(frames, rows, length_ref)
    trim_row = trim_ref[...].astype(F32)
    kept = jnp.where(member, BLOCK * (end_row - frame) - trim_row, 0.0)
    limit[...] = jnp.broadcast_to(jnp.sum(kept, axis=1, keepdims=True), limit.shape)


def first_kernel(first_ref, kernel1):
    taps = first_ref.shape[0]
    first = first_ref[...]
    first = first - jnp.mean(first, axis=-1, keepdims=True)
    first = jnp.concatenate([first, jnp.zeros((16 - taps, first.shape[1]), F32)], axis=0)
    high, low = two_parts(first)
    kernel1[...] = jnp.zeros_like(kernel1)
    kernel1[0:16, :] = high
    kernel1[64:80, :] = low
    kernel1[128:144, :] = high


def unpack(n, packing, rows, recv, limit, highs, lows):
    cap, stride = packing.cap, packing.stride
    frames = limit.shape[0]

    def take(r):
        return recv[pl.ds(r, n, stride=stride), :]

    meta = take(packing.meta)
    lane = iota((n, LANES), 1)
    half = LANES // 2
    base = lax.axis_index("dp").astype(F32) * rows + 1.0
    frame = iota((n, LANES), 1)
    zeros = jnp.zeros((n, LANES), F32)
    picks, data = [], []
    for i in range(cap):
        slot = jnp.sum(jnp.where(lane == float(LOOK + i), meta, 0.0), axis=1, keepdims=True)
        picks.append(jnp.where((slot - base == frame) & (frame < float(rows)), 1.0, 0.0))
        pair = take(2 * cap + i // 2)
        data.append(jnp.concatenate([take(i), take(cap + i), pair if i % 2 == 0 else pltpu.roll(pair, half, 1)], axis=1))
    picks.append(jnp.where(frame == float(rows), 1.0, 0.0))
    data.append(jnp.concatenate([jnp.where(lane < float(LOOK), meta, 0.0), zeros, zeros], axis=1))
    high, low = two_parts(jnp.concatenate(data, axis=0))
    pick = jnp.concatenate(picks, axis=0).astype(BF16)
    spread = lax.dot_general(
        pick, jnp.concatenate([high, low], axis=1), (((0,), (0,)), ((), ())), preferred_element_type=F32
    )[:frames]
    lane = iota((frames, LANES), 1)
    left = lane < float(half)
    for part, out in ((0, highs), (1, lows)):
        tiles = []
        for t in range(3):
            tile = spread[:, (3 * part + t) * LANES : (3 * part + t + 1) * LANES]
            tiles.append(jnp.where(lane + float(t * LANES) < limit[...], tile, 0.0))
        behind = pltpu.roll(pltpu.roll(tiles[0], frames - 1, 0), half, 1)
        tiles[2] = jnp.where(left, tiles[2], behind)
        for j in range(BLOCK // 40):
            t, at = divmod(40 * j, LANES)
            window = tiles[t]
            if at > half:
                window = jnp.where(lane >= float(at), window, tiles[t + 1])
            plain = pltpu.roll(window, LANES - at, 1) if at else window
            if part == 0:
                plain = jnp.where(left, plain, pltpu.roll(window, (LANES - at + half) % LANES, 1))
            out[j, :, :] = plain


def convs(rows, highs, lows, kernel1, mid_ref, tail_ref, out_ref, work):
    (e1, o1, e2, o2, e3, o3, e4, o4, e5, o5, e6, o6, halo1, halo2, halo3, halo4,
     acc1, acc2, acc3, acc4, acc5, acc6, acc7) = work

    def windows(k):
        j, o = divmod(k, 8)
        parts = [highs[j, :rows, :], lows[j, :rows, :]]
        if o:
            parts = [pltpu.roll(part, LANES - 5 * o, 1) for part in parts]
        return jnp.concatenate(parts, axis=1).astype(BF16)

    def halo_windows():
        line = lax.broadcasted_iota(jnp.int32, (16, LANES), 0)
        totals = [jnp.zeros((16, LANES), F32)] * 2
        for k in range(16):
            j, o = divmod(k, 8)
            row = k // 2 + 8 * (k % 2)
            for index, part in enumerate((highs, lows)):
                block = jnp.broadcast_to(part[j, rows : rows + 1, :], (16, LANES))
                if o:
                    block = pltpu.roll(block, LANES - 5 * o, 1)
                totals[index] = jnp.where(line == row, block, totals[index])
        return jnp.concatenate(totals, axis=1).astype(BF16)

    def split(chunk):
        first, last = (0, 16) if chunk == 0 else (16 * chunk + 1, min(16 * chunk + 16, 63))
        return list(range(first, last + 1))

    def multiply1(chunk):
        phases = split(chunk)
        acc = acc1[chunk % 2]
        for s in range(0, len(phases), 4):
            group = phases[s : s + 4]
            blocks = [windows(k) for k in group]
            size = len(group) * rows
            if chunk == 0 and s + 4 >= len(phases):
                blocks.append(halo_windows())
                size += 16
            acc[s * rows : s * rows + size, :] = jnp.dot(
                jnp.concatenate(blocks, axis=0), kernel1[...], preferred_element_type=F32
            )

    def finish1(chunk):
        phases = split(chunk)
        acc = acc1[chunk % 2]
        if chunk == 0:
            at = len(phases) * rows
            halo1[0:16, :] = unit_gelu(acc[at : at + 16, :], EPS)
        for index, k in enumerate(phases):
            dest = e1 if k % 2 == 0 else o1
            for r in range(0, rows, 16):
                block = acc[index * rows + r : index * rows + r + 16, :]
                dest[k // 2 * rows + r : k // 2 * rows + r + 16, :] = unit_gelu(block, EPS).astype(BF16)

    def halo_row(halo):
        return jnp.concatenate([halo[c, 0:1, :] for c in range(halo.shape[0])], axis=1)

    def wrap(even, halo, blocks):
        rolled = pltpu.roll(even[:rows, :].astype(F32), rows - 1, 0)
        last = lax.broadcasted_iota(jnp.int32, rolled.shape, 0) == rows - 1
        even[blocks * rows : (blocks + 1) * rows, :] = jnp.where(last, halo, rolled).astype(BF16)

    def halo_taps(halo, interleaved):
        if interleaved:
            pieces = halo.shape[0]
            taps = [
                jnp.concatenate([halo[c, pl.ds(offset, 8, stride=2), :] for c in range(pieces)], axis=1)
                for offset in range(3)
            ]
        else:
            taps = [halo[0:8, :], halo[8:16, :], pltpu.roll(halo[0:8, :], 7, 0)]
        taps = [jnp.concatenate([tap, jnp.zeros_like(tap)], axis=0).astype(BF16) for tap in taps]
        return jnp.concatenate(taps, axis=1)

    def multiply(even, odd, weight, taps, first, phases, acc, halo=None):
        at, size = first * rows, phases * rows
        inputs = [even[at : at + size, :], odd[at : at + size, :]]
        if taps == 3:
            inputs.append(even[at + rows : at + rows + size, :])
        left = jnp.concatenate(inputs, axis=1)
        if halo is not None:
            left = jnp.concatenate([left, halo], axis=0)
        acc[: left.shape[0], :] = jnp.dot(left, weight[...], preferred_element_type=F32)

    def finish(first, phases, acc, dest_even, dest_odd, halo=None):
        if halo is not None:
            at = phases * rows
            ends = norm_unit_gelu(acc[at : at + 16, :], 2.0 * EPS)
            for c in range(halo.shape[0]):
                halo[c, 0:8, :] = ends[:8, c * LANES : (c + 1) * LANES]
        for p in range(phases):
            k = first + p
            dest = dest_even if k % 2 == 0 else dest_odd
            for r in range(0, rows, 16):
                block = acc[p * rows + r : p * rows + r + 16, :]
                dest[k // 2 * rows + r : k // 2 * rows + r + 16, :] = norm_unit_gelu(block, 2.0 * EPS).astype(BF16)

    mids = [mid_ref.at[i] for i in range(4)]
    tails = [tail_ref.at[i] for i in range(2)]
    for halo in (halo2, halo3, halo4):
        halo[...] = jnp.zeros_like(halo)

    def multiply2(c):
        multiply(e1, o1, mids[0], 3, 8 * c, 8, acc2[c % 2], halo_taps(halo1, False) if c == 0 else None)

    def finish2(c):
        finish(8 * c, 8, acc2[c % 2], e2, o2, halo2 if c == 0 else None)

    def multiply3(c):
        multiply(e2, o2, mids[1], 3, 8 * c, 8, acc3[c % 2], halo_taps(halo2, True) if c == 0 else None)

    def finish3(c):
        finish(8 * c, 8, acc3[c % 2], e3, o3, halo3 if c == 0 else None)

    multiply1(0)
    multiply1(1)
    finish1(0)
    multiply2(0)
    multiply1(2)
    finish1(1)
    wrap(e1, halo1[0:1, :], 32)
    multiply2(1)
    multiply1(3)
    finish1(2)
    finish2(0)
    wrap(e2, halo_row(halo2), 16)
    multiply2(2)
    finish1(3)
    finish2(1)
    multiply2(3)
    finish2(2)
    multiply3(0)
    finish2(3)
    multiply3(1)
    finish3(0)
    wrap(e3, halo_row(halo3), 8)
    finish3(1)
    multiply(e3, o3, mids[2], 3, 0, 8, acc4, halo_taps(halo3, True))
    finish(0, 8, acc4, e4, o4, halo4)
    wrap(e4, halo_row(halo4), 4)
    multiply(e4, o4, mids[3], 3, 0, 4, acc5)
    finish(0, 4, acc5, e5, o5)
    multiply(e5, o5, tails[0], 2, 0, 2, acc6)
    finish(0, 2, acc6, e6, o6)
    multiply(e6, o6, tails[1], 2, 0, 1, acc7)
    for r in range(0, rows, 16):
        out_ref[r : r + 16, :] = (norm_unit_gelu(acc7[r : r + 16, :], 2.0 * EPS) * HALF_ROOT).astype(BF16)


def means(n, reach, feature_ref, length_ref, out_ref, send, recv, send_sem, recv_sem):
    me = lax.axis_index("dp")
    rows, channels = feature_ref.shape
    pieces = channels // LANES
    links = [(k, k - 1) for k in range(1, reach + 1)] + [(-k, reach + k - 1) for k in range(1, reach + 1)]

    def inside(k):
        return (me + k < n) & (me + k >= 0)

    base = me.astype(F32) * rows
    _, _, start_col, end_col, _ = spans(rows, rows, length_ref)
    start_row = to_row(start_col)
    end_row = to_row(end_col)
    features = feature_ref[...]
    line = iota((16, rows), 1) + base
    last = line >= start_row[:, rows - 1 : rows]
    initial = line < end_row[:, 0:1]
    pick = jnp.where(iota((16, rows), 0) == 0.0, jnp.where(last, 1.0, 0.0), jnp.where(initial, 1.0, 0.0))
    edges = jnp.dot(pick.astype(BF16), features, preferred_element_type=F32)
    for index in range(2):
        for piece in range(pieces):
            send[index, piece : piece + 1, :] = edges[index : index + 1, piece * LANES : (piece + 1) * LANES]

    def copy(k, slot):
        return pltpu.make_async_remote_copy(
            src_ref=send.at[0 if k > 0 else 1],
            dst_ref=recv.at[slot],
            send_sem=send_sem.at[slot],
            recv_sem=recv_sem.at[slot],
            device_id={"dp": me + k},
        )

    for k, slot in links:
        @pl.when(inside(k))
        def _():
            copy(k, slot).start()
    local = iota((rows, rows), 1) + base
    within = jnp.where((start_col <= local) & (local < end_col), 1.0, 0.0).astype(BF16)
    totals = jnp.dot(within, features, preferred_element_type=F32)
    for k, slot in links:
        @pl.when(inside(-k))
        def _():
            copy(-k, slot).wait_recv()

        @pl.when(inside(k))
        def _():
            copy(k, slot).wait_send()
    for k, slot in links:
        row = jnp.concatenate([recv[slot, piece : piece + 1, :] for piece in range(pieces)], axis=1)
        if k > 0:
            reached = start_col <= base - (k - 1) * rows - 1.0
        else:
            reached = end_col > base - k * rows
        totals = totals + jnp.where(reached, row, 0.0)
    out_ref[...] = (features.astype(F32) - totals / (end_col - start_col)).astype(BF16)


def frontend_kernel(
    n, packing, reach,
    wave_hbm, slot_hbm, length_hbm, trim_hbm, first_hbm, mid_hbm, tail_hbm, out_ref,
    wave, slot, length, trim, first, load_sem,
    send, recv, send_sem, recv_sem,
    mid, tail, weight_sem, features, edges, far, edge_send_sem, edge_recv_sem,
    limit, kernel1, highs, lows, *work,
):
    small = [
        pltpu.make_async_copy(source, target, load_sem.at[i])
        for i, (source, target) in enumerate(
            ((slot_hbm, slot), (wave_hbm, wave), (length_hbm, length), (trim_hbm, trim), (first_hbm, first))
        )
    ]
    for load in small:
        load.start()
    greet(n)
    loads = [pltpu.make_async_copy(mid_hbm.at[i], mid.at[i], weight_sem.at[i]) for i in range(4)]
    loads.append(pltpu.make_async_copy(tail_hbm, tail, weight_sem.at[4]))
    for load in loads:
        load.start()
    rows = wave.shape[0]
    far[...] = jnp.zeros_like(far)
    edges[...] = jnp.zeros_like(edges)
    small[0].wait()
    small[1].wait()
    pack(n, packing, wave, slot, send)
    scatter(n, packing.stride, send, recv, send_sem, recv_sem)
    small[2].wait()
    small[3].wait()
    small[4].wait()
    keep_limit(limit.shape[0], rows, length, trim, limit)
    first_kernel(first, kernel1)
    gather(n, packing.stride, send, recv, send_sem, recv_sem)
    for load in loads:
        load.wait()
    unpack(n, packing, rows, recv, limit, highs, lows)
    split = iter(work)
    single = [next(split) for _ in range(16)]
    accs = [[next(split), next(split)] for _ in range(3)] + list(split)
    convs(rows, highs, lows, kernel1, mid, tail, features, single + accs)
    means(n, reach, features, length, out_ref, edges, far, edge_send_sem, edge_recv_sem)


def per_device(wave, row_slot, frame_lengths, sample_trim, first_weight, mid_weight, tail_weight):
    rows = wave.shape[0]
    taps, channels = first_weight.shape
    rolls = frame_lengths.shape[0]
    n = lax.axis_size("dp")
    packing = Packing(rows // n + 2)
    reach = min((MAXLEN + rows - 2) // rows, n - 1)
    mid = mid_weight.reshape(4, 3 * channels, channels)
    tail = tail_weight.reshape(2, 2 * channels, channels)
    vmem = pl.BlockSpec(memory_space=pltpu.VMEM)
    outside = pl.BlockSpec(memory_space=pl.ANY)
    message = (n * packing.stride, LANES)
    frames = rows + 16

    def slab(phases):
        return pltpu.VMEM((phases * rows, channels), BF16)

    halo = pltpu.VMEM((channels // LANES, 24, LANES), F32)

    def total(size):
        return pltpu.VMEM((size, channels), F32)

    return pl.pallas_call(
        functools.partial(frontend_kernel, n, packing, reach),
        out_shape=jax.ShapeDtypeStruct((rows, channels), BF16),
        in_specs=[outside] * 7,
        out_specs=vmem,
        scratch_shapes=[
            pltpu.VMEM(wave.shape, F32),
            pltpu.VMEM((1, rows), jnp.int32),
            pltpu.VMEM((1, rolls), jnp.int32),
            pltpu.VMEM((1, rolls), jnp.int32),
            pltpu.VMEM((taps, channels), F32),
            pltpu.SemaphoreType.DMA((5,)),
            pltpu.VMEM(message, F32),
            pltpu.VMEM(message, F32),
            pltpu.SemaphoreType.DMA((n,)),
            pltpu.SemaphoreType.DMA((n,)),
            pltpu.VMEM(mid.shape, BF16),
            pltpu.VMEM(tail.shape, BF16),
            pltpu.SemaphoreType.DMA((5,)),
            pltpu.VMEM((rows, channels), BF16),
            pltpu.VMEM((2, 8, LANES), F32),
            pltpu.VMEM((2 * reach, 8, LANES), F32),
            pltpu.SemaphoreType.DMA((2 * reach,)),
            pltpu.SemaphoreType.DMA((2 * reach,)),
            pltpu.VMEM((frames, LANES), F32),
            pltpu.VMEM((2 * LANES, channels), BF16),
            pltpu.VMEM((BLOCK // 40, frames, LANES), F32),
            pltpu.VMEM((BLOCK // 40, frames, LANES), F32),
            slab(33), slab(32), slab(17), slab(16), slab(9), slab(8), slab(5), slab(4),
            slab(2), slab(2), slab(1), slab(1),
            total(16), halo, halo, halo,
            total(17 * rows + 16), total(17 * rows + 16),
            total(8 * rows + 16), total(8 * rows + 16),
            total(8 * rows + 16), total(8 * rows + 16),
            total(8 * rows + 16), total(4 * rows), total(2 * rows), total(rows),
        ],
        compiler_params=pltpu.CompilerParams(
            collective_id=0, has_side_effects=True, vmem_limit_bytes=64 * 1024 * 1024 - 64 * 1024
        ),
        name="frontend",
    )(
        wave, row_slot.reshape(1, -1), frame_lengths.reshape(1, -1), sample_trim.reshape(1, -1),
        first_weight, mid, tail,
    )


def solution(mesh):
    placed = (
        P(("groups", "dp"), None),
        P(("groups", "dp")),
        P("groups"),
        P("groups"),
        P(),
        P(),
        P(),
    )
    return jax.shard_map(
        per_device, mesh=mesh, in_specs=placed, out_specs=P(("groups", "dp"), None), check_vma=False
    )
```

```python
import functools

import jax
import jax.numpy as jnp
from jax import lax
from jax.experimental import pallas as pl
from jax.experimental.pallas import tpu as pltpu
from jax.sharding import PartitionSpec as P

BLOCK = 320
LOOK = 80
LANES = 128
MAXLEN = 256
EPS = 1e-05
HALF_ROOT = 0.7071067811865476
F32 = jnp.float32
BF16 = jnp.bfloat16


def iota(shape, dim):
    return lax.broadcasted_iota(jnp.int32, shape, dim).astype(F32)


def to_column(row):
    size = row.shape[1]
    same = iota((size, size), 0) == iota((size, size), 1)
    return jnp.sum(jnp.where(same, row, 0.0), axis=1, keepdims=True)


def to_row(column):
    size = column.shape[0]
    same = iota((size, size), 0) == iota((size, size), 1)
    return jnp.sum(jnp.where(same, column, 0.0), axis=0, keepdims=True)


def two_parts(values):
    high = values.astype(BF16)
    return high, (values - high.astype(F32)).astype(BF16)


def unit_gelu(centred, eps):
    spread = jnp.mean(centred * centred, axis=-1, keepdims=True)
    scaled = centred * (lax.rsqrt(spread + eps) * HALF_ROOT)
    return scaled + scaled * lax.erf(scaled)


def norm_unit_gelu(values, eps):
    return unit_gelu(values - jnp.mean(values, axis=-1, keepdims=True), eps)


class Packing:
    def __init__(self, cap):
        self.cap = cap
        self.pairs = (cap + 1) // 2
        self.meta = 2 * cap + self.pairs
        self.stride = (self.meta + 1 + 7) // 8 * 8


def choose(n, packing, slot_ref, pick, marks):
    rows = slot_ref.shape[1]
    cap, stride = packing.cap, packing.stride
    slot_row = slot_ref[...].astype(F32)
    slot_col = to_column(slot_row)
    target_row = jnp.floor(slot_row / rows)
    target_col = jnp.floor(slot_col / rows)
    alike = target_col == target_row
    earlier = iota((rows, rows), 0) < iota((rows, rows), 1)
    later = iota((rows, rows), 0) > iota((rows, rows), 1)
    rank_row = jnp.sum(jnp.where(earlier & alike, 1.0, 0.0), axis=0, keepdims=True)
    rank_col = jnp.sum(jnp.where(later & alike, 1.0, 0.0), axis=1, keepdims=True)
    base = target_row * stride
    half_rank = jnp.floor(rank_row / 2.0)
    odd = rank_row - 2.0 * half_rank == 1.0
    pair = base + 2 * cap + half_rank
    ahead = jnp.where(target_row * rows == slot_row, base - stride + packing.meta, -1.0)
    places = [
        base + rank_row,
        base + cap + rank_row,
        jnp.where(odd, -1.0, pair),
        jnp.where(odd, pair, -1.0),
        ahead,
        base + packing.meta,
    ]
    place = iota((n * stride, rows), 0)
    pick[...] = jnp.concatenate([jnp.where(place == p, 1.0, 0.0) for p in places], axis=1).astype(BF16)
    marks[...] = jnp.where(iota((rows, LANES), 1) == LOOK + rank_col, slot_col + 1.0, 0.0)


def pack(wave_ref, pick, marks, send):
    rows = wave_ref.shape[0]
    lane = iota((rows, LANES), 1)
    tile0 = wave_ref[:, :LANES]
    tile1 = wave_ref[:, LANES : 2 * LANES]
    rest = jnp.concatenate([wave_ref[:, 2 * LANES : BLOCK], jnp.zeros((rows, 3 * LANES - BLOCK), F32)], axis=1)
    blocks = [
        tile0, tile1, rest, pltpu.roll(rest, LANES // 2, 1), jnp.where(lane < LOOK, tile0, 0.0), marks[...],
    ]
    high, low = two_parts(jnp.concatenate(blocks, axis=0))
    send[...] = jnp.dot(pick[...], high, preferred_element_type=F32) + jnp.dot(
        pick[...], low, preferred_element_type=F32
    )


def greet(n):
    me = lax.axis_index("dp")

    def one(to, carry):
        pl.semaphore_signal(pltpu.get_barrier_semaphore(), inc=1, device_id={"dp": to})
        return carry

    lax.fori_loop(me + 1, n, one, 0)


def exchange(n, stride, send, recv, send_sem, recv_sem, in_sem):
    me = lax.axis_index("dp")
    mine = pl.ds(pl.multiple_of(me * stride, stride), stride)

    def outgoing(to):
        return pltpu.make_async_remote_copy(
            src_ref=send.at[pl.ds(pl.multiple_of(to * stride, stride), stride)],
            dst_ref=recv.at[mine],
            send_sem=send_sem.at[to],
            recv_sem=recv_sem.at[me],
            device_id={"dp": to},
        )

    def incoming(source):
        return pltpu.make_async_remote_copy(
            src_ref=send.at[mine],
            dst_ref=recv.at[pl.ds(pl.multiple_of(source * stride, stride), stride)],
            send_sem=send_sem.at[source],
            recv_sem=recv_sem.at[source],
            device_id={"dp": source},
        )

    def enter():
        @pl.when(me > 0)
        def _():
            pl.semaphore_wait(pltpu.get_barrier_semaphore(), me)

        def one(to, carry):
            pl.semaphore_signal(in_sem.at[me], inc=1, device_id={"dp": to})
            return carry

        lax.fori_loop(0, me, one, 0)

    def begin():
        recv[mine, :] = send[mine, :]

        def one(to, carry):
            outgoing(to).start()
            return carry

        lax.fori_loop(0, me, one, 0)

    def finish():
        def above(to, carry):
            pl.semaphore_wait(in_sem.at[to], 1)
            outgoing(to).start()
            return carry

        def arrive(other, carry):
            incoming(other).wait_recv()
            return carry

        lax.fori_loop(me + 1, n, above, 0)
        lax.fori_loop(me + 1, n, arrive, 0)
        lax.fori_loop(0, me, arrive, 0)

    def drain():
        def one(other, carry):
            outgoing(other).wait_send()
            return carry

        lax.fori_loop(0, me, one, 0)
        lax.fori_loop(me + 1, n, one, 0)

    return enter, begin, finish, drain


def spans(frames, rows, length_ref):
    first = lax.axis_index("dp").astype(F32) * rows
    length_row = length_ref[...].astype(F32)
    count = length_row.shape[1]
    length_col = to_column(length_row)
    before = iota((count, count), 0) < iota((count, count), 1)
    start_row = jnp.sum(jnp.where(before, length_col, 0.0), axis=0, keepdims=True)
    end_row = start_row + length_row
    frame = iota((frames, count), 0) + first
    member = (start_row <= frame) & (frame < end_row)
    start = jnp.sum(jnp.where(member, start_row, 0.0), axis=1, keepdims=True)
    end = jnp.sum(jnp.where(member, end_row, 0.0), axis=1, keepdims=True)
    return member, frame, start, end, end_row


def keep_limit(frames, rows, length_ref, trim_ref, limit):
    member, frame, _, _, end_row = spans(frames, rows, length_ref)
    trim_row = trim_ref[...].astype(F32)
    kept = jnp.where(member, BLOCK * (end_row - frame) - trim_row, 0.0)
    limit[...] = jnp.broadcast_to(jnp.sum(kept, axis=1, keepdims=True), limit.shape)


def first_kernel(first_ref, kernel1):
    taps = first_ref.shape[0]
    first = first_ref[...]
    first = first - jnp.mean(first, axis=-1, keepdims=True)
    first = jnp.concatenate([first, jnp.zeros((16 - taps, first.shape[1]), F32)], axis=0)
    high, low = two_parts(first)
    kernel1[...] = jnp.zeros_like(kernel1)
    kernel1[0:16, :] = high
    kernel1[64:80, :] = low
    kernel1[128:144, :] = high


def unpack(n, packing, rows, recv, limit, highs, lows):
    cap, stride = packing.cap, packing.stride
    frames = limit.shape[0]

    def take(r):
        return recv[pl.ds(r, n, stride=stride), :]

    meta = take(packing.meta)
    lane = iota((n, LANES), 1)
    half = LANES // 2
    base = lax.axis_index("dp").astype(F32) * rows + 1.0
    frame = iota((n, LANES), 1)
    zeros = jnp.zeros((n, LANES), F32)
    picks, data = [], []
    for i in range(cap):
        slot = jnp.sum(jnp.where(lane == float(LOOK + i), meta, 0.0), axis=1, keepdims=True)
        picks.append(jnp.where((slot - base == frame) & (frame < float(rows)), 1.0, 0.0))
        pair = take(2 * cap + i // 2)
        data.append(jnp.concatenate([take(i), take(cap + i), pair if i % 2 == 0 else pltpu.roll(pair, half, 1)], axis=1))
    picks.append(jnp.where(frame == float(rows), 1.0, 0.0))
    data.append(jnp.concatenate([jnp.where(lane < float(LOOK), meta, 0.0), zeros, zeros], axis=1))
    high, low = two_parts(jnp.concatenate(data, axis=0))
    pick = jnp.concatenate(picks, axis=0).astype(BF16)
    spread = lax.dot_general(
        pick, jnp.concatenate([high, low], axis=1), (((0,), (0,)), ((), ())), preferred_element_type=F32
    )[:frames]
    lane = iota((frames, LANES), 1)
    left = lane < float(half)
    for part, out in ((0, highs), (1, lows)):
        tiles = []
        for t in range(3):
            tile = spread[:, (3 * part + t) * LANES : (3 * part + t + 1) * LANES]
            tiles.append(jnp.where(lane + float(t * LANES) < limit[...], tile, 0.0))
        behind = pltpu.roll(pltpu.roll(tiles[0], frames - 1, 0), half, 1)
        tiles[2] = jnp.where(left, tiles[2], behind)
        for j in range(BLOCK // 40):
            t, at = divmod(40 * j, LANES)
            window = tiles[t]
            if at > half:
                window = jnp.where(lane >= float(at), window, tiles[t + 1])
            plain = pltpu.roll(window, LANES - at, 1) if at else window
            if part == 0:
                plain = jnp.where(left, plain, pltpu.roll(window, (LANES - at + half) % LANES, 1))
            out[j, :, :] = plain


def convs(rows, highs, lows, kernel1, mid_ref, tail_ref, out_ref, work):
    (e1, o1, e2, o2, e3, o3, e4, o4, e5, o5, e6, o6, halo1, halo2, halo3, halo4,
     acc1, acc2, acc3, acc4, acc5, acc6, acc7) = work

    def windows(k):
        j, o = divmod(k, 8)
        parts = [highs[j, :rows, :], lows[j, :rows, :]]
        if o:
            parts = [pltpu.roll(part, LANES - 5 * o, 1) for part in parts]
        return jnp.concatenate(parts, axis=1).astype(BF16)

    def halo_windows():
        line = lax.broadcasted_iota(jnp.int32, (16, LANES), 0)
        totals = [jnp.zeros((16, LANES), F32)] * 2
        for k in range(16):
            j, o = divmod(k, 8)
            row = k // 2 + 8 * (k % 2)
            for index, part in enumerate((highs, lows)):
                block = jnp.broadcast_to(part[j, rows : rows + 1, :], (16, LANES))
                if o:
                    block = pltpu.roll(block, LANES - 5 * o, 1)
                totals[index] = jnp.where(line == row, block, totals[index])
        return jnp.concatenate(totals, axis=1).astype(BF16)

    def split(chunk):
        first, last = (0, 16) if chunk == 0 else (16 * chunk + 1, min(16 * chunk + 16, 63))
        return list(range(first, last + 1))

    def multiply1(chunk):
        phases = split(chunk)
        acc = acc1[chunk % 2]
        for s in range(0, len(phases), 4):
            group = phases[s : s + 4]
            blocks = [windows(k) for k in group]
            size = len(group) * rows
            if chunk == 0 and s + 4 >= len(phases):
                blocks.append(halo_windows())
                size += 16
            acc[s * rows : s * rows + size, :] = jnp.dot(
                jnp.concatenate(blocks, axis=0), kernel1[...], preferred_element_type=F32
            )

    def finish1(chunk):
        phases = split(chunk)
        acc = acc1[chunk % 2]
        if chunk == 0:
            at = len(phases) * rows
            halo1[0:16, :] = unit_gelu(acc[at : at + 16, :], EPS)
        for index, k in enumerate(phases):
            dest = e1 if k % 2 == 0 else o1
            for r in range(0, rows, 16):
                block = acc[index * rows + r : index * rows + r + 16, :]
                dest[k // 2 * rows + r : k // 2 * rows + r + 16, :] = unit_gelu(block, EPS).astype(BF16)

    def halo_row(halo):
        return jnp.concatenate([halo[c, 0:1, :] for c in range(halo.shape[0])], axis=1)

    def wrap(even, halo, blocks):
        rolled = pltpu.roll(even[:rows, :].astype(F32), rows - 1, 0)
        last = lax.broadcasted_iota(jnp.int32, rolled.shape, 0) == rows - 1
        even[blocks * rows : (blocks + 1) * rows, :] = jnp.where(last, halo, rolled).astype(BF16)

    def halo_taps(halo, interleaved):
        if interleaved:
            pieces = halo.shape[0]
            taps = [
                jnp.concatenate([halo[c, pl.ds(offset, 8, stride=2), :] for c in range(pieces)], axis=1)
                for offset in range(3)
            ]
        else:
            taps = [halo[0:8, :], halo[8:16, :], pltpu.roll(halo[0:8, :], 7, 0)]
        taps = [jnp.concatenate([tap, jnp.zeros_like(tap)], axis=0).astype(BF16) for tap in taps]
        return jnp.concatenate(taps, axis=1)

    def multiply(even, odd, weight, taps, first, phases, acc, halo=None):
        at, size = first * rows, phases * rows
        inputs = [even[at : at + size, :], odd[at : at + size, :]]
        if taps == 3:
            inputs.append(even[at + rows : at + rows + size, :])
        left = jnp.concatenate(inputs, axis=1)
        if halo is not None:
            left = jnp.concatenate([left, halo], axis=0)
        acc[: left.shape[0], :] = jnp.dot(left, weight[...], preferred_element_type=F32)

    def finish(first, phases, acc, dest_even, dest_odd, halo=None):
        if halo is not None:
            at = phases * rows
            ends = norm_unit_gelu(acc[at : at + 16, :], 2.0 * EPS)
            for c in range(halo.shape[0]):
                halo[c, 0:8, :] = ends[:8, c * LANES : (c + 1) * LANES]
        for p in range(phases):
            k = first + p
            dest = dest_even if k % 2 == 0 else dest_odd
            for r in range(0, rows, 16):
                block = acc[p * rows + r : p * rows + r + 16, :]
                dest[k // 2 * rows + r : k // 2 * rows + r + 16, :] = norm_unit_gelu(block, 2.0 * EPS).astype(BF16)

    mids = [mid_ref.at[i] for i in range(4)]
    tails = [tail_ref.at[i] for i in range(2)]
    for halo in (halo2, halo3, halo4):
        halo[...] = jnp.zeros_like(halo)

    def multiply2(c):
        multiply(e1, o1, mids[0], 3, 8 * c, 8, acc2[c % 2], halo_taps(halo1, False) if c == 0 else None)

    def finish2(c):
        finish(8 * c, 8, acc2[c % 2], e2, o2, halo2 if c == 0 else None)

    def multiply3(c):
        multiply(e2, o2, mids[1], 3, 8 * c, 8, acc3[c % 2], halo_taps(halo2, True) if c == 0 else None)

    def finish3(c):
        finish(8 * c, 8, acc3[c % 2], e3, o3, halo3 if c == 0 else None)

    multiply1(0)
    multiply1(1)
    finish1(0)
    multiply2(0)
    multiply1(2)
    finish1(1)
    wrap(e1, halo1[0:1, :], 32)
    multiply2(1)
    multiply1(3)
    finish1(2)
    finish2(0)
    wrap(e2, halo_row(halo2), 16)
    multiply2(2)
    finish1(3)
    finish2(1)
    multiply2(3)
    finish2(2)
    multiply3(0)
    finish2(3)
    multiply3(1)
    finish3(0)
    wrap(e3, halo_row(halo3), 8)
    finish3(1)
    multiply(e3, o3, mids[2], 3, 0, 8, acc4, halo_taps(halo3, True))
    finish(0, 8, acc4, e4, o4, halo4)
    wrap(e4, halo_row(halo4), 4)
    multiply(e4, o4, mids[3], 3, 0, 4, acc5)
    finish(0, 4, acc5, e5, o5)
    multiply(e5, o5, tails[0], 2, 0, 2, acc6)
    finish(0, 2, acc6, e6, o6)
    multiply(e6, o6, tails[1], 2, 0, 1, acc7)
    for r in range(0, rows, 16):
        out_ref[r : r + 16, :] = (norm_unit_gelu(acc7[r : r + 16, :], 2.0 * EPS) * HALF_ROOT).astype(BF16)


def means(n, reach, feature_ref, length_ref, out_ref, send, recv, send_sem, recv_sem, drain):
    me = lax.axis_index("dp")
    rows, channels = feature_ref.shape
    pieces = channels // LANES
    links = [(k, k - 1) for k in range(1, reach + 1)] + [(-k, reach + k - 1) for k in range(1, reach + 1)]

    def inside(k):
        return (me + k < n) & (me + k >= 0)

    base = me.astype(F32) * rows
    _, _, start_col, end_col, _ = spans(rows, rows, length_ref)
    start_row = to_row(start_col)
    end_row = to_row(end_col)
    features = feature_ref[...]
    line = iota((16, rows), 1) + base
    last = line >= start_row[:, rows - 1 : rows]
    initial = line < end_row[:, 0:1]
    pick = jnp.where(iota((16, rows), 0) == 0.0, jnp.where(last, 1.0, 0.0), jnp.where(initial, 1.0, 0.0))
    edges = jnp.dot(pick.astype(BF16), features, preferred_element_type=F32)
    for index in range(2):
        for piece in range(pieces):
            send[index, piece : piece + 1, :] = edges[index : index + 1, piece * LANES : (piece + 1) * LANES]

    def copy(k, slot):
        return pltpu.make_async_remote_copy(
            src_ref=send.at[0 if k > 0 else 1],
            dst_ref=recv.at[slot],
            send_sem=send_sem.at[slot],
            recv_sem=recv_sem.at[slot],
            device_id={"dp": me + k},
        )

    for k, slot in links:
        @pl.when(inside(k))
        def _():
            copy(k, slot).start()
    local = iota((rows, rows), 1) + base
    within = jnp.where((start_col <= local) & (local < end_col), 1.0, 0.0).astype(BF16)
    totals = jnp.dot(within, features, preferred_element_type=F32)
    drain()
    for k, slot in links:
        @pl.when(inside(-k))
        def _():
            copy(-k, slot).wait_recv()

        @pl.when(inside(k))
        def _():
            copy(k, slot).wait_send()
    for k, slot in links:
        row = jnp.concatenate([recv[slot, piece : piece + 1, :] for piece in range(pieces)], axis=1)
        if k > 0:
            reached = start_col <= base - (k - 1) * rows - 1.0
        else:
            reached = end_col > base - k * rows
        totals = totals + jnp.where(reached, row, 0.0)
    out_ref[...] = (features.astype(F32) - totals / (end_col - start_col)).astype(BF16)


def frontend_kernel(
    n, packing, reach,
    wave_hbm, slot_hbm, length_hbm, trim_hbm, first_hbm, mid_hbm, tail_hbm, out_ref,
    wave, slot, length, trim, first, load_sem, pick, marks,
    send, recv, send_sem, recv_sem, in_sem,
    mid, tail, weight_sem, features, edges, far, edge_send_sem, edge_recv_sem,
    limit, kernel1, highs, lows, *work,
):
    small = [
        pltpu.make_async_copy(source, target, load_sem.at[i])
        for i, (source, target) in enumerate(
            ((slot_hbm, slot), (wave_hbm, wave), (length_hbm, length), (trim_hbm, trim), (first_hbm, first))
        )
    ]
    for load in small:
        load.start()
    greet(n)
    loads = [pltpu.make_async_copy(mid_hbm.at[i], mid.at[i], weight_sem.at[i]) for i in range(4)]
    loads.append(pltpu.make_async_copy(tail_hbm, tail, weight_sem.at[4]))
    for load in loads:
        load.start()
    rows = wave.shape[0]
    far[...] = jnp.zeros_like(far)
    edges[...] = jnp.zeros_like(edges)
    enter, begin, finish, drain = exchange(n, packing.stride, send, recv, send_sem, recv_sem, in_sem)
    small[0].wait()
    choose(n, packing, slot, pick, marks)
    enter()
    small[1].wait()
    pack(wave, pick, marks, send)
    begin()
    small[2].wait()
    small[3].wait()
    small[4].wait()
    keep_limit(limit.shape[0], rows, length, trim, limit)
    first_kernel(first, kernel1)
    finish()
    for load in loads:
        load.wait()
    unpack(n, packing, rows, recv, limit, highs, lows)
    split = iter(work)
    single = [next(split) for _ in range(16)]
    accs = [[next(split), next(split)] for _ in range(3)] + list(split)
    convs(rows, highs, lows, kernel1, mid, tail, features, single + accs)
    means(n, reach, features, length, out_ref, edges, far, edge_send_sem, edge_recv_sem, drain)


def per_device(wave, row_slot, frame_lengths, sample_trim, first_weight, mid_weight, tail_weight):
    rows = wave.shape[0]
    taps, channels = first_weight.shape
    rolls = frame_lengths.shape[0]
    n = lax.axis_size("dp")
    packing = Packing(rows // n + 2)
    reach = min((MAXLEN + rows - 2) // rows, n - 1)
    mid = mid_weight.reshape(4, 3 * channels, channels)
    tail = tail_weight.reshape(2, 2 * channels, channels)
    vmem = pl.BlockSpec(memory_space=pltpu.VMEM)
    outside = pl.BlockSpec(memory_space=pl.ANY)
    message = (n * packing.stride, LANES)
    frames = rows + 16

    def slab(phases):
        return pltpu.VMEM((phases * rows, channels), BF16)

    halo = pltpu.VMEM((channels // LANES, 24, LANES), F32)

    def total(size):
        return pltpu.VMEM((size, channels), F32)

    return pl.pallas_call(
        functools.partial(frontend_kernel, n, packing, reach),
        out_shape=pltpu.VMEM((rows, channels), BF16),
        in_specs=[outside] * 7,
        out_specs=vmem,
        scratch_shapes=[
            pltpu.VMEM(wave.shape, F32),
            pltpu.VMEM((1, rows), jnp.int32),
            pltpu.VMEM((1, rolls), jnp.int32),
            pltpu.VMEM((1, rolls), jnp.int32),
            pltpu.VMEM((taps, channels), F32),
            pltpu.SemaphoreType.DMA((5,)),
            pltpu.VMEM((message[0], 6 * rows), BF16),
            pltpu.VMEM((rows, LANES), F32),
            pltpu.VMEM(message, F32),
            pltpu.VMEM(message, F32),
            pltpu.SemaphoreType.DMA((n,)),
            pltpu.SemaphoreType.DMA((n,)),
            pltpu.SemaphoreType.REGULAR((n,)),
            pltpu.VMEM(mid.shape, BF16),
            pltpu.VMEM(tail.shape, BF16),
            pltpu.SemaphoreType.DMA((5,)),
            pltpu.VMEM((rows, channels), BF16),
            pltpu.VMEM((2, 8, LANES), F32),
            pltpu.VMEM((2 * reach, 8, LANES), F32),
            pltpu.SemaphoreType.DMA((2 * reach,)),
            pltpu.SemaphoreType.DMA((2 * reach,)),
            pltpu.VMEM((frames, LANES), F32),
            pltpu.VMEM((2 * LANES, channels), BF16),
            pltpu.VMEM((BLOCK // 40, frames, LANES), F32),
            pltpu.VMEM((BLOCK // 40, frames, LANES), F32),
            slab(33), slab(32), slab(17), slab(16), slab(9), slab(8), slab(5), slab(4),
            slab(2), slab(2), slab(1), slab(1),
            total(16), halo, halo, halo,
            total(17 * rows + 16), total(17 * rows + 16),
            total(8 * rows + 16), total(8 * rows + 16),
            total(8 * rows + 16), total(8 * rows + 16),
            total(8 * rows + 16), total(4 * rows), total(2 * rows), total(rows),
        ],
        compiler_params=pltpu.CompilerParams(
            collective_id=0, has_side_effects=True, vmem_limit_bytes=48 * 1024 * 1024
        ),
        name="frontend",
    )(*[pltpu.with_memory_space_constraint(x, pltpu.HBM) for x in (
        wave, row_slot.reshape(1, -1), frame_lengths.reshape(1, -1), sample_trim.reshape(1, -1),
        first_weight, mid, tail)]
    )


def solution(mesh):
    placed = (
        P(("groups", "dp"), None),
        P(("groups", "dp")),
        P("groups"),
        P("groups"),
        P(),
        P(),
        P(),
    )
    return jax.shard_map(
        per_device, mesh=mesh, in_specs=placed, out_specs=P(("groups", "dp"), None), check_vma=False
    )
```

```python
import functools

import jax
import jax.numpy as jnp
from jax import lax
from jax.experimental import pallas as pl
from jax.experimental.pallas import tpu as pltpu
from jax.sharding import PartitionSpec as P

BLOCK = 320
LOOK = 80
LANES = 128
STEP = 20
MAXLEN = 256
EPS = 1e-05
HALF_ROOT = 0.7071067811865476
F32 = jnp.float32
BF16 = jnp.bfloat16


def iota(shape, dim):
    return lax.broadcasted_iota(jnp.int32, shape, dim).astype(F32)


def to_column(row):
    size = row.shape[1]
    same = iota((size, size), 0) == iota((size, size), 1)
    return jnp.sum(jnp.where(same, row, 0.0), axis=1, keepdims=True)


def to_row(column):
    size = column.shape[0]
    same = iota((size, size), 0) == iota((size, size), 1)
    return jnp.sum(jnp.where(same, column, 0.0), axis=0, keepdims=True)


def two_parts(values):
    high = values.astype(BF16)
    return high, (values - high.astype(F32)).astype(BF16)


def unit_gelu(centred, eps):
    total = jnp.sum(centred * centred, axis=-1, keepdims=True)
    scaled = centred * lax.rsqrt(total * (2.0 / centred.shape[-1]) + 2.0 * eps)
    return scaled + scaled * lax.erf(scaled)


def norm_unit_gelu(values, eps):
    return unit_gelu(values - jnp.mean(values, axis=-1, keepdims=True), eps)


class Packing:
    def __init__(self, cap):
        self.cap = cap
        self.pairs = (cap + 1) // 2
        self.meta = 2 * cap + self.pairs
        self.stride = (self.meta + 1 + 7) // 8 * 8


def choose(n, packing, slot_ref, pick, marks):
    rows = slot_ref.shape[1]
    cap, stride = packing.cap, packing.stride
    slot_row = slot_ref[...].astype(F32)
    slot_col = to_column(slot_row)
    target_row = jnp.floor(slot_row / rows)
    target_col = jnp.floor(slot_col / rows)
    alike = target_col == target_row
    earlier = iota((rows, rows), 0) < iota((rows, rows), 1)
    later = iota((rows, rows), 0) > iota((rows, rows), 1)
    rank_row = jnp.sum(jnp.where(earlier & alike, 1.0, 0.0), axis=0, keepdims=True)
    rank_col = jnp.sum(jnp.where(later & alike, 1.0, 0.0), axis=1, keepdims=True)
    base = target_row * stride
    half_rank = jnp.floor(rank_row / 2.0)
    odd = rank_row - 2.0 * half_rank == 1.0
    pair = base + 2 * cap + half_rank
    ahead = jnp.where(target_row * rows == slot_row, base - stride + packing.meta, -1.0)
    places = [
        base + rank_row,
        base + cap + rank_row,
        jnp.where(odd, -1.0, pair),
        jnp.where(odd, pair, -1.0),
        ahead,
        base + packing.meta,
    ]
    place = iota((n * stride, rows), 0)
    pick[...] = jnp.concatenate([jnp.where(place == p, 1.0, 0.0) for p in places], axis=1).astype(BF16)
    marks[...] = jnp.where(iota((rows, LANES), 1) == LOOK + rank_col, slot_col + 1.0, 0.0)


def pack(wave_ref, pick, marks, send):
    rows = wave_ref.shape[0]
    lane = iota((rows, LANES), 1)
    tile0 = wave_ref[:, :LANES]
    tile1 = wave_ref[:, LANES : 2 * LANES]
    rest = jnp.concatenate([wave_ref[:, 2 * LANES : BLOCK], jnp.zeros((rows, 3 * LANES - BLOCK), F32)], axis=1)
    blocks = [
        tile0, tile1, rest, pltpu.roll(rest, LANES // 2, 1), jnp.where(lane < LOOK, tile0, 0.0), marks[...],
    ]
    high, low = two_parts(jnp.concatenate(blocks, axis=0))
    send[...] = jnp.dot(pick[...], high, preferred_element_type=F32) + jnp.dot(
        pick[...], low, preferred_element_type=F32
    )


def greet(n):
    me = lax.axis_index("dp")

    def one(to, carry):
        pl.semaphore_signal(pltpu.get_barrier_semaphore(), inc=1, device_id={"dp": to})
        return carry

    lax.fori_loop(me + 1, n, one, 0)


def exchange(n, stride, send, recv, send_sem, recv_sem, in_sem):
    me = lax.axis_index("dp")
    mine = pl.ds(pl.multiple_of(me * stride, stride), stride)

    def outgoing(to):
        return pltpu.make_async_remote_copy(
            src_ref=send.at[pl.ds(pl.multiple_of(to * stride, stride), stride)],
            dst_ref=recv.at[mine],
            send_sem=send_sem.at[to],
            recv_sem=recv_sem.at[me],
            device_id={"dp": to},
        )

    def incoming(source):
        return pltpu.make_async_remote_copy(
            src_ref=send.at[mine],
            dst_ref=recv.at[pl.ds(pl.multiple_of(source * stride, stride), stride)],
            send_sem=send_sem.at[source],
            recv_sem=recv_sem.at[source],
            device_id={"dp": source},
        )

    def enter():
        @pl.when(me > 0)
        def _():
            pl.semaphore_wait(pltpu.get_barrier_semaphore(), me)

    def begin():
        def one(to, carry):
            outgoing(to).start()
            return carry

        def tell(to, carry):
            pl.semaphore_signal(in_sem.at[me], inc=1, device_id={"dp": to})
            return carry

        lax.fori_loop(0, me, one, 0)
        lax.fori_loop(0, me, tell, 0)
        recv[mine, :] = send[mine, :]

    def finish():
        def above(to, carry):
            pl.semaphore_wait(in_sem.at[to], 1)
            outgoing(to).start()
            return carry

        def arrive(other, carry):
            incoming(other).wait_recv()
            return carry

        lax.fori_loop(me + 1, n, above, 0)
        lax.fori_loop(me + 1, n, arrive, 0)
        lax.fori_loop(0, me, arrive, 0)

    def drain():
        def one(other, carry):
            outgoing(other).wait_send()
            return carry

        lax.fori_loop(0, me, one, 0)
        lax.fori_loop(me + 1, n, one, 0)

    return enter, begin, finish, drain


def spans(frames, rows, length_ref):
    first = lax.axis_index("dp").astype(F32) * rows
    length_row = length_ref[...].astype(F32)
    count = length_row.shape[1]
    length_col = to_column(length_row)
    before = iota((count, count), 0) < iota((count, count), 1)
    start_row = jnp.sum(jnp.where(before, length_col, 0.0), axis=0, keepdims=True)
    end_row = start_row + length_row
    frame = iota((frames, count), 0) + first
    member = (start_row <= frame) & (frame < end_row)
    start = jnp.sum(jnp.where(member, start_row, 0.0), axis=1, keepdims=True)
    end = jnp.sum(jnp.where(member, end_row, 0.0), axis=1, keepdims=True)
    return member, frame, start, end, end_row


def keep_limit(frames, rows, length_ref, trim_ref, limit):
    member, frame, _, _, end_row = spans(frames, rows, length_ref)
    trim_row = trim_ref[...].astype(F32)
    kept = jnp.where(member, BLOCK * (end_row - frame) - trim_row, 0.0)
    limit[...] = jnp.broadcast_to(jnp.sum(kept, axis=1, keepdims=True), limit.shape)


def first_kernel(first_ref, kernel1):
    taps = first_ref.shape[0]
    first = first_ref[...]
    first = first - jnp.mean(first, axis=-1, keepdims=True)
    first = jnp.concatenate([first, jnp.zeros((16 - taps, first.shape[1]), F32)], axis=0)
    high, low = two_parts(first)
    kernel1[...] = jnp.zeros_like(kernel1)
    kernel1[0:16, :] = high
    kernel1[32:48, :] = low
    kernel1[64:80, :] = high


def unpack(n, packing, rows, recv, limit, views):
    cap, stride = packing.cap, packing.stride
    frames = limit.shape[0]

    def take(r):
        return recv[pl.ds(r, n, stride=stride), :]

    meta = take(packing.meta)
    lane = iota((n, LANES), 1)
    half = LANES // 2
    base = lax.axis_index("dp").astype(F32) * rows + 1.0
    frame = iota((n, LANES), 1)
    zeros = jnp.zeros((n, LANES), F32)
    picks, data = [], []
    for i in range(cap):
        slot = jnp.sum(jnp.where(lane == float(LOOK + i), meta, 0.0), axis=1, keepdims=True)
        picks.append(jnp.where((slot - base == frame) & (frame < float(rows)), 1.0, 0.0))
        pair = take(2 * cap + i // 2)
        data.append(jnp.concatenate([take(i), take(cap + i), pair if i % 2 == 0 else pltpu.roll(pair, half, 1)], axis=1))
    picks.append(jnp.where(frame == float(rows), 1.0, 0.0))
    data.append(jnp.concatenate([jnp.where(lane < float(LOOK), meta, 0.0), zeros, zeros], axis=1))
    high, low = two_parts(jnp.concatenate(data, axis=0))
    pick = jnp.concatenate(picks, axis=0).astype(BF16)
    spread = lax.dot_general(
        pick, jnp.concatenate([high, low], axis=1), (((0,), (0,)), ((), ())), preferred_element_type=F32
    )[:frames]
    lane = iota((frames, LANES), 1)
    left = lane < float(half)
    parts = []
    for part in range(2):
        tiles = []
        for t in range(3):
            tile = spread[:, (3 * part + t) * LANES : (3 * part + t + 1) * LANES]
            tiles.append(jnp.where(lane + float(t * LANES) < limit[...], tile, 0.0))
        behind = pltpu.roll(pltpu.roll(tiles[0], frames - 1, 0), half, 1)
        tiles[2] = jnp.where(left, tiles[2], behind)
        parts.append(tiles)
    for j in range(BLOCK // STEP):
        t, at = divmod(STEP * j, LANES)

        def window(part, place):
            tile = parts[part][t]
            if at + 32 > LANES:
                tile = jnp.where(lane >= float(at), tile, parts[part][t + 1])
            shift = (LANES - at + place) % LANES
            return pltpu.roll(tile, shift, 1) if shift else tile

        inner = jnp.where(lane < 32.0, window(0, 0), window(0, 32))
        views[j, :, :] = jnp.where(left, inner, window(1, 64))


def convs(rows, views, kernel1, mid_ref, tail_ref, out_ref, work):
    (e1, o1, e2, o2, e3, o3, e4, o4, e5, o5, e6, o6, halo1, halo2, halo3, halo4,
     acc1, acc2, acc3, acc4, acc5, acc6, acc7) = work

    def windows(k):
        j, o = divmod(5 * k, STEP)
        view = views[j, :rows, :]
        return (pltpu.roll(view, LANES - o, 1) if o else view).astype(BF16)

    def halo_windows():
        line = lax.broadcasted_iota(jnp.int32, (16, LANES), 0)
        total = jnp.zeros((16, LANES), F32)
        for k in range(16):
            j, o = divmod(5 * k, STEP)
            block = jnp.broadcast_to(views[j, rows : rows + 1, :], (16, LANES))
            if o:
                block = pltpu.roll(block, LANES - o, 1)
            total = jnp.where(line == k // 2 + 8 * (k % 2), block, total)
        return total.astype(BF16)

    def split(chunk):
        first, last = (0, 16) if chunk == 0 else (16 * chunk + 1, min(16 * chunk + 16, 63))
        return list(range(first, last + 1))

    def multiply1(chunk):
        phases = split(chunk)
        acc = acc1[chunk % 2]
        for s in range(0, len(phases), 4):
            group = phases[s : s + 4]
            blocks = [windows(k) for k in group]
            size = len(group) * rows
            if chunk == 0 and s + 4 >= len(phases):
                blocks.append(halo_windows())
                size += 16
            acc[s * rows : s * rows + size, :] = jnp.dot(
                jnp.concatenate(blocks, axis=0), kernel1[...], preferred_element_type=F32
            )

    def finish1(chunk):
        phases = split(chunk)
        acc = acc1[chunk % 2]
        if chunk == 0:
            at = len(phases) * rows
            halo1[0:16, :] = unit_gelu(acc[at : at + 16, :], EPS)
        for index, k in enumerate(phases):
            dest = e1 if k % 2 == 0 else o1
            for r in range(0, rows, 16):
                block = acc[index * rows + r : index * rows + r + 16, :]
                dest[k // 2 * rows + r : k // 2 * rows + r + 16, :] = unit_gelu(block, EPS).astype(BF16)

    def halo_row(halo):
        return jnp.concatenate([halo[c, 0:1, :] for c in range(halo.shape[0])], axis=1)

    def wrap(even, halo, blocks):
        rolled = pltpu.roll(even[:rows, :].astype(F32), rows - 1, 0)
        last = lax.broadcasted_iota(jnp.int32, rolled.shape, 0) == rows - 1
        even[blocks * rows : (blocks + 1) * rows, :] = jnp.where(last, halo, rolled).astype(BF16)

    def halo_taps(halo, interleaved):
        if interleaved:
            pieces = halo.shape[0]
            taps = [
                jnp.concatenate([halo[c, pl.ds(offset, 8, stride=2), :] for c in range(pieces)], axis=1)
                for offset in range(3)
            ]
        else:
            taps = [halo[0:8, :], halo[8:16, :], pltpu.roll(halo[0:8, :], 7, 0)]
        taps = [jnp.concatenate([tap, jnp.zeros_like(tap)], axis=0).astype(BF16) for tap in taps]
        return jnp.concatenate(taps, axis=1)

    def multiply(even, odd, weight, taps, first, phases, acc, halo=None):
        at, size = first * rows, phases * rows
        inputs = [even[at : at + size, :], odd[at : at + size, :]]
        if taps == 3:
            inputs.append(even[at + rows : at + rows + size, :])
        left = jnp.concatenate(inputs, axis=1)
        if halo is not None:
            left = jnp.concatenate([left, halo], axis=0)
        acc[: left.shape[0], :] = jnp.dot(left, weight[...], preferred_element_type=F32)

    def finish(first, phases, acc, dest_even, dest_odd, halo=None):
        if halo is not None:
            at = phases * rows
            ends = norm_unit_gelu(acc[at : at + 16, :], 2.0 * EPS)
            for c in range(halo.shape[0]):
                halo[c, 0:8, :] = ends[:8, c * LANES : (c + 1) * LANES]
        for p in range(phases):
            k = first + p
            dest = dest_even if k % 2 == 0 else dest_odd
            for r in range(0, rows, 16):
                block = acc[p * rows + r : p * rows + r + 16, :]
                dest[k // 2 * rows + r : k // 2 * rows + r + 16, :] = norm_unit_gelu(block, 2.0 * EPS).astype(BF16)

    mids = [mid_ref.at[i] for i in range(4)]
    tails = [tail_ref.at[i] for i in range(2)]
    for halo in (halo2, halo3, halo4):
        halo[...] = jnp.zeros_like(halo)

    layers = {
        2: (e1, o1, e2, o2, mids[0], 3, acc2, halo1, halo2, 16),
        3: (e2, o2, e3, o3, mids[1], 3, acc3, halo2, halo3, 8),
        4: (e3, o3, e4, o4, mids[2], 3, acc4, halo3, halo4, 4),
        5: (e4, o4, e5, o5, mids[3], 3, acc5, None, None, 0),
        6: (e5, o5, e6, o6, tails[0], 2, acc6, None, None, 0),
    }

    def m(layer, first, last, slot):
        even, odd, _, _, weight, taps, acc, halo, _, _ = layers[layer]
        halo = halo_taps(halo, layer > 2) if halo is not None and first == 0 else None
        multiply(even, odd, weight, taps, first, last - first, acc[slot], halo)

    def f(layer, first, last, slot):
        _, _, even, odd, _, _, acc, _, halo, blocks = layers[layer]
        halo = halo if first == 0 else None
        finish(first, last - first, acc[slot], even, odd, halo)
        if halo is not None:
            wrap(even, halo_row(halo), blocks)

    multiply1(0)
    multiply1(1)
    finish1(0)
    m(2, 0, 8, 0)
    multiply1(2)
    finish1(1)
    wrap(e1, halo1[0:1, :], 32)
    m(2, 8, 16, 1)
    multiply1(3)
    finish1(2)
    f(2, 0, 8, 0)
    m(2, 16, 24, 0)
    finish1(3)
    f(2, 8, 16, 1)
    m(2, 24, 32, 1)
    f(2, 16, 24, 0)
    m(3, 0, 11, 0)
    f(2, 24, 32, 1)
    m(3, 11, 16, 1)
    f(3, 0, 11, 0)
    m(4, 0, 5, 0)
    f(3, 11, 16, 1)
    m(4, 5, 8, 1)
    f(4, 0, 5, 0)
    m(5, 0, 2, 0)
    f(4, 5, 8, 1)
    m(5, 2, 4, 1)
    f(5, 0, 2, 0)
    m(6, 0, 1, 0)
    f(5, 2, 4, 1)
    m(6, 1, 2, 1)
    f(6, 0, 1, 0)
    f(6, 1, 2, 1)
    multiply(e6, o6, tails[1], 2, 0, 1, acc7)
    for r in range(0, rows, 16):
        out_ref[r : r + 16, :] = (norm_unit_gelu(acc7[r : r + 16, :], 2.0 * EPS) * HALF_ROOT).astype(BF16)


def means(n, reach, feature_ref, length_ref, out_ref, send, recv, send_sem, recv_sem, drain):
    me = lax.axis_index("dp")
    rows, channels = feature_ref.shape
    pieces = channels // LANES
    links = [(k, k - 1) for k in range(1, reach + 1)] + [(-k, reach + k - 1) for k in range(1, reach + 1)]

    def inside(k):
        return (me + k < n) & (me + k >= 0)

    base = me.astype(F32) * rows
    _, _, start_col, end_col, _ = spans(rows, rows, length_ref)
    start_row = to_row(start_col)
    end_row = to_row(end_col)
    features = feature_ref[...]
    line = iota((16, rows), 1) + base
    last = line >= start_row[:, rows - 1 : rows]
    initial = line < end_row[:, 0:1]
    pick = jnp.where(iota((16, rows), 0) == 0.0, jnp.where(last, 1.0, 0.0), jnp.where(initial, 1.0, 0.0))
    edges = jnp.dot(pick.astype(BF16), features, preferred_element_type=F32)
    for index in range(2):
        for piece in range(pieces):
            send[index, piece : piece + 1, :] = edges[index : index + 1, piece * LANES : (piece + 1) * LANES]

    def copy(k, slot):
        return pltpu.make_async_remote_copy(
            src_ref=send.at[0 if k > 0 else 1],
            dst_ref=recv.at[slot],
            send_sem=send_sem.at[slot],
            recv_sem=recv_sem.at[slot],
            device_id={"dp": me + k},
        )

    for k, slot in links:
        @pl.when(inside(k))
        def _():
            copy(k, slot).start()
    local = iota((rows, rows), 1) + base
    within = jnp.where((start_col <= local) & (local < end_col), 1.0, 0.0).astype(BF16)
    totals = jnp.dot(within, features, preferred_element_type=F32)
    share = 1.0 / (end_col - start_col)
    from_below = start_col < base
    from_above = end_col > base + rows
    first_start, last_end = start_row[:, 0:1], end_row[:, rows - 1 : rows]
    drain()
    for k, slot in links:
        @pl.when(inside(-k))
        def _():
            copy(-k, slot).wait_recv()
    below = jnp.zeros((8, LANES), F32)
    above = jnp.zeros((8, LANES), F32)
    for k, slot in links:
        if k > 0:
            below = below + jnp.where(first_start <= base - (k - 1) * rows - 1.0, recv[slot], 0.0)
        else:
            above = above + jnp.where(last_end > base - k * rows, recv[slot], 0.0)

    def widen(tile):
        return jnp.concatenate([tile[piece : piece + 1, :] for piece in range(pieces)], axis=1)

    totals = totals + jnp.where(from_below, widen(below), 0.0) + jnp.where(from_above, widen(above), 0.0)
    out_ref[...] = (features.astype(F32) - totals * share).astype(BF16)
    for k, slot in links:
        @pl.when(inside(k))
        def _():
            copy(k, slot).wait_send()


def frontend_kernel(
    n, packing, reach,
    wave_hbm, slot_hbm, length_hbm, trim_hbm, first_hbm, mid_hbm, tail_hbm, out_ref,
    wave, slot, length, trim, first, load_sem, pick, marks,
    send, recv, send_sem, recv_sem, in_sem,
    mid, tail, weight_sem, features, edges, far, edge_send_sem, edge_recv_sem,
    limit, kernel1, views, *work,
):
    small = [
        pltpu.make_async_copy(source, target, load_sem.at[i])
        for i, (source, target) in enumerate(
            ((slot_hbm, slot), (wave_hbm, wave), (length_hbm, length), (trim_hbm, trim), (first_hbm, first))
        )
    ]
    for load in small:
        load.start()
    greet(n)
    loads = [pltpu.make_async_copy(mid_hbm.at[i], mid.at[i], weight_sem.at[i]) for i in range(4)]
    loads.append(pltpu.make_async_copy(tail_hbm, tail, weight_sem.at[4]))
    for load in loads:
        load.start()
    rows = wave.shape[0]
    far[...] = jnp.zeros_like(far)
    edges[...] = jnp.zeros_like(edges)
    enter, begin, finish, drain = exchange(n, packing.stride, send, recv, send_sem, recv_sem, in_sem)
    small[0].wait()
    choose(n, packing, slot, pick, marks)
    enter()
    small[1].wait()
    pack(wave, pick, marks, send)
    begin()
    small[2].wait()
    small[3].wait()
    small[4].wait()
    keep_limit(limit.shape[0], rows, length, trim, limit)
    first_kernel(first, kernel1)
    finish()
    for load in loads:
        load.wait()
    unpack(n, packing, rows, recv, limit, views)
    split = iter(work)
    single = [next(split) for _ in range(16)]
    accs = [[next(split), next(split)] for _ in range(6)] + list(split)
    convs(rows, views, kernel1, mid, tail, features, single + accs)
    means(n, reach, features, length, out_ref, edges, far, edge_send_sem, edge_recv_sem, drain)


def per_device(wave, row_slot, frame_lengths, sample_trim, first_weight, mid_weight, tail_weight):
    rows = wave.shape[0]
    taps, channels = first_weight.shape
    rolls = frame_lengths.shape[0]
    n = lax.axis_size("dp")
    packing = Packing(rows // n + 2)
    reach = min((MAXLEN + rows - 2) // rows, n - 1)
    mid = mid_weight.reshape(4, 3 * channels, channels)
    tail = tail_weight.reshape(2, 2 * channels, channels)
    vmem = pl.BlockSpec(memory_space=pltpu.VMEM)
    outside = pl.BlockSpec(memory_space=pl.ANY)
    message = (n * packing.stride, LANES)
    frames = rows + 16

    def slab(phases):
        return pltpu.VMEM((phases * rows, channels), BF16)

    halo = pltpu.VMEM((channels // LANES, 24, LANES), F32)

    def total(size):
        return pltpu.VMEM((size, channels), F32)

    return pl.pallas_call(
        functools.partial(frontend_kernel, n, packing, reach),
        out_shape=pltpu.VMEM((rows, channels), BF16),
        in_specs=[outside] * 7,
        out_specs=vmem,
        scratch_shapes=[
            pltpu.VMEM(wave.shape, F32),
            pltpu.VMEM((1, rows), jnp.int32),
            pltpu.VMEM((1, rolls), jnp.int32),
            pltpu.VMEM((1, rolls), jnp.int32),
            pltpu.VMEM((taps, channels), F32),
            pltpu.SemaphoreType.DMA((5,)),
            pltpu.VMEM((message[0], 6 * rows), BF16),
            pltpu.VMEM((rows, LANES), F32),
            pltpu.VMEM(message, F32),
            pltpu.VMEM(message, F32),
            pltpu.SemaphoreType.DMA((n,)),
            pltpu.SemaphoreType.DMA((n,)),
            pltpu.SemaphoreType.REGULAR((n,)),
            pltpu.VMEM(mid.shape, BF16),
            pltpu.VMEM(tail.shape, BF16),
            pltpu.SemaphoreType.DMA((5,)),
            pltpu.VMEM((rows, channels), BF16),
            pltpu.VMEM((2, 8, LANES), F32),
            pltpu.VMEM((2 * reach, 8, LANES), F32),
            pltpu.SemaphoreType.DMA((2 * reach,)),
            pltpu.SemaphoreType.DMA((2 * reach,)),
            pltpu.VMEM((frames, LANES), F32),
            pltpu.VMEM((LANES, channels), BF16),
            pltpu.VMEM((BLOCK // STEP, frames, LANES), F32),
            slab(33), slab(32), slab(17), slab(16), slab(9), slab(8), slab(5), slab(4),
            slab(2), slab(2), slab(1), slab(1),
            total(16), halo, halo, halo,
            total(17 * rows + 16), total(17 * rows + 16),
            total(8 * rows + 16), total(8 * rows + 16),
            total(11 * rows + 16), total(5 * rows),
            total(5 * rows + 16), total(3 * rows),
            total(4 * rows), total(2 * rows),
            total(2 * rows), total(rows),
            total(rows),
        ],
        compiler_params=pltpu.CompilerParams(
            collective_id=0, has_side_effects=True, vmem_limit_bytes=48 * 1024 * 1024
        ),
        name="frontend",
    )(*[pltpu.with_memory_space_constraint(x, pltpu.HBM) for x in (
        wave, row_slot.reshape(1, -1), frame_lengths.reshape(1, -1), sample_trim.reshape(1, -1),
        first_weight, mid, tail)]
    )


def solution(mesh):
    placed = (
        P(("groups", "dp"), None),
        P(("groups", "dp")),
        P("groups"),
        P("groups"),
        P(),
        P(),
        P(),
    )
    return jax.shard_map(
        per_device, mesh=mesh, in_specs=placed, out_specs=P(("groups", "dp"), None), check_vma=False
    )
```

```python
import functools

import jax
import jax.numpy as jnp
from jax import lax
from jax.experimental import pallas as pl
from jax.experimental.pallas import tpu as pltpu
from jax.sharding import PartitionSpec as P

BLOCK = 320
LOOK = 80
LANES = 128
STEP = 20
MAXLEN = 256
EPS = 1e-05
HALF_ROOT = 0.7071067811865476
F32 = jnp.float32
BF16 = jnp.bfloat16


def iota(shape, dim):
    return lax.broadcasted_iota(jnp.int32, shape, dim).astype(F32)


def to_column(row):
    size = row.shape[1]
    same = iota((size, size), 0) == iota((size, size), 1)
    return jnp.sum(jnp.where(same, row, 0.0), axis=1, keepdims=True)


def to_row(column):
    size = column.shape[0]
    same = iota((size, size), 0) == iota((size, size), 1)
    return jnp.sum(jnp.where(same, column, 0.0), axis=0, keepdims=True)


def two_parts(values):
    high = values.astype(BF16)
    return high, (values - high.astype(F32)).astype(BF16)


def unit_gelu(centred, eps):
    total = jnp.sum(centred * centred, axis=-1, keepdims=True)
    scaled = centred * lax.rsqrt(total * (2.0 / centred.shape[-1]) + 2.0 * eps)
    return scaled + scaled * lax.erf(scaled)


def norm_unit_gelu(values, eps):
    return unit_gelu(values - jnp.mean(values, axis=-1, keepdims=True), eps)


class Packing:
    def __init__(self, cap):
        self.cap = cap
        self.pairs = (cap + 1) // 2
        self.meta = 2 * cap + self.pairs
        self.stride = (self.meta + 1 + 7) // 8 * 8


def choose(n, packing, slot_ref, pick, marks):
    rows = slot_ref.shape[1]
    cap, stride = packing.cap, packing.stride
    slot_row = slot_ref[...].astype(F32)
    slot_col = to_column(slot_row)
    target_row = jnp.floor(slot_row / rows)
    target_col = jnp.floor(slot_col / rows)
    alike = target_col == target_row
    earlier = iota((rows, rows), 0) < iota((rows, rows), 1)
    later = iota((rows, rows), 0) > iota((rows, rows), 1)
    rank_row = jnp.sum(jnp.where(earlier & alike, 1.0, 0.0), axis=0, keepdims=True)
    rank_col = jnp.sum(jnp.where(later & alike, 1.0, 0.0), axis=1, keepdims=True)
    base = target_row * stride
    half_rank = jnp.floor(rank_row / 2.0)
    odd = rank_row - 2.0 * half_rank == 1.0
    pair = base + 2 * cap + half_rank
    ahead = jnp.where(target_row * rows == slot_row, base - stride + packing.meta, -1.0)
    places = [
        base + rank_row,
        base + cap + rank_row,
        jnp.where(odd, -1.0, pair),
        jnp.where(odd, pair, -1.0),
        ahead,
        base + packing.meta,
    ]
    place = iota((n * stride, rows), 0)
    pick[...] = jnp.concatenate([jnp.where(place == p, 1.0, 0.0) for p in places], axis=1).astype(BF16)
    marks[...] = jnp.where(iota((rows, LANES), 1) == LOOK + rank_col, slot_col + 1.0, 0.0)


def pack(wave_ref, pick, marks, send):
    rows = wave_ref.shape[0]
    lane = iota((rows, LANES), 1)
    tile0 = wave_ref[:, :LANES]
    tile1 = wave_ref[:, LANES : 2 * LANES]
    rest = jnp.concatenate([wave_ref[:, 2 * LANES : BLOCK], jnp.zeros((rows, 3 * LANES - BLOCK), F32)], axis=1)
    blocks = [
        tile0, tile1, rest, pltpu.roll(rest, LANES // 2, 1), jnp.where(lane < LOOK, tile0, 0.0), marks[...],
    ]
    high, low = two_parts(jnp.concatenate(blocks, axis=0))
    send[...] = jnp.dot(pick[...], high, preferred_element_type=F32) + jnp.dot(
        pick[...], low, preferred_element_type=F32
    )


def greet(n):
    me = lax.axis_index("dp")

    def one(to, carry):
        pl.semaphore_signal(pltpu.get_barrier_semaphore(), inc=1, device_id={"dp": to})
        return carry

    lax.fori_loop(me + 1, n, one, 0)


def exchange(n, stride, send, recv, send_sem, recv_sem, in_sem):
    me = lax.axis_index("dp")
    mine = pl.ds(pl.multiple_of(me * stride, stride), stride)

    def outgoing(to):
        return pltpu.make_async_remote_copy(
            src_ref=send.at[pl.ds(pl.multiple_of(to * stride, stride), stride)],
            dst_ref=recv.at[mine],
            send_sem=send_sem.at[to],
            recv_sem=recv_sem.at[me],
            device_id={"dp": to},
        )

    def incoming(source):
        return pltpu.make_async_remote_copy(
            src_ref=send.at[mine],
            dst_ref=recv.at[pl.ds(pl.multiple_of(source * stride, stride), stride)],
            send_sem=send_sem.at[source],
            recv_sem=recv_sem.at[source],
            device_id={"dp": source},
        )

    def enter():
        @pl.when(me > 0)
        def _():
            pl.semaphore_wait(pltpu.get_barrier_semaphore(), me)

    def begin():
        def one(to, carry):
            outgoing(to).start()
            return carry

        def tell(to, carry):
            pl.semaphore_signal(in_sem.at[me], inc=1, device_id={"dp": to})
            return carry

        lax.fori_loop(0, me, one, 0)
        lax.fori_loop(0, me, tell, 0)
        recv[mine, :] = send[mine, :]

    def finish():
        def above(to, carry):
            pl.semaphore_wait(in_sem.at[to], 1)
            outgoing(to).start()
            return carry

        def arrive(other, carry):
            incoming(other).wait_recv()
            return carry

        lax.fori_loop(me + 1, n, above, 0)
        lax.fori_loop(me + 1, n, arrive, 0)
        lax.fori_loop(0, me, arrive, 0)

    def drain():
        def one(other, carry):
            outgoing(other).wait_send()
            return carry

        lax.fori_loop(0, me, one, 0)
        lax.fori_loop(me + 1, n, one, 0)

    return enter, begin, finish, drain


def spans(frames, rows, length_ref):
    first = lax.axis_index("dp").astype(F32) * rows
    length_row = length_ref[...].astype(F32)
    count = length_row.shape[1]
    length_col = to_column(length_row)
    before = iota((count, count), 0) < iota((count, count), 1)
    start_row = jnp.sum(jnp.where(before, length_col, 0.0), axis=0, keepdims=True)
    end_row = start_row + length_row
    frame = iota((frames, count), 0) + first
    member = (start_row <= frame) & (frame < end_row)
    start = jnp.sum(jnp.where(member, start_row, 0.0), axis=1, keepdims=True)
    end = jnp.sum(jnp.where(member, end_row, 0.0), axis=1, keepdims=True)
    return member, frame, start, end, end_row


def keep_limit(frames, rows, length_ref, trim_ref, limit):
    member, frame, _, _, end_row = spans(frames, rows, length_ref)
    trim_row = trim_ref[...].astype(F32)
    kept = jnp.where(member, BLOCK * (end_row - frame) - trim_row, 0.0)
    limit[...] = jnp.broadcast_to(jnp.sum(kept, axis=1, keepdims=True), limit.shape)


def first_kernel(first_ref, kernel1):
    taps = first_ref.shape[0]
    first = first_ref[...]
    first = first - jnp.mean(first, axis=-1, keepdims=True)
    first = jnp.concatenate([first, jnp.zeros((16 - taps, first.shape[1]), F32)], axis=0)
    high, low = two_parts(first)
    kernel1[...] = jnp.zeros_like(kernel1)
    kernel1[0:16, :] = high
    kernel1[32:48, :] = low
    kernel1[64:80, :] = high


def unpack(n, packing, rows, recv, limit, views):
    cap, stride = packing.cap, packing.stride
    frames = limit.shape[0]

    def take(r):
        return recv[pl.ds(r, n, stride=stride), :]

    meta = take(packing.meta)
    lane = iota((n, LANES), 1)
    half = LANES // 2
    base = lax.axis_index("dp").astype(F32) * rows + 1.0
    frame = iota((n, LANES), 1)
    zeros = jnp.zeros((n, LANES), F32)
    picks, data = [], []
    for i in range(cap):
        slot = jnp.sum(jnp.where(lane == float(LOOK + i), meta, 0.0), axis=1, keepdims=True)
        picks.append(jnp.where((slot - base == frame) & (frame < float(rows)), 1.0, 0.0))
        pair = take(2 * cap + i // 2)
        data.append(jnp.concatenate([take(i), take(cap + i), pair if i % 2 == 0 else pltpu.roll(pair, half, 1)], axis=1))
    picks.append(jnp.where(frame == float(rows), 1.0, 0.0))
    data.append(jnp.concatenate([jnp.where(lane < float(LOOK), meta, 0.0), zeros, zeros], axis=1))
    high, low = two_parts(jnp.concatenate(data, axis=0))
    pick = jnp.concatenate(picks, axis=0).astype(BF16)
    spread = lax.dot_general(
        pick, jnp.concatenate([high, low], axis=1), (((0,), (0,)), ((), ())), preferred_element_type=F32
    )[:frames]
    lane = iota((frames, LANES), 1)
    left = lane < float(half)
    parts = []
    for part in range(2):
        tiles = []
        for t in range(3):
            tile = spread[:, (3 * part + t) * LANES : (3 * part + t + 1) * LANES]
            tiles.append(jnp.where(lane + float(t * LANES) < limit[...], tile, 0.0))
        behind = pltpu.roll(pltpu.roll(tiles[0], frames - 1, 0), half, 1)
        tiles[2] = jnp.where(left, tiles[2], behind)
        parts.append(tiles)
    for j in range(BLOCK // STEP):
        t, at = divmod(STEP * j, LANES)

        def window(part, place):
            tile = parts[part][t]
            if at + 32 > LANES:
                tile = jnp.where(lane >= float(at), tile, parts[part][t + 1])
            shift = (LANES - at + place) % LANES
            return pltpu.roll(tile, shift, 1) if shift else tile

        inner = jnp.where(lane < 32.0, window(0, 0), window(0, 32))
        views[j, :, :] = jnp.where(left, inner, window(1, 64))


def convs(rows, views, kernel1, mid_ref, tail_ref, out_ref, work):
    (e1, o1, e2, o2, e3, o3, e4, o4, e5, o5, e6, o6, halo1, halo2, halo3, halo4,
     acc1, acc2, acc3, acc4, acc5, acc6, acc7) = work

    def windows(k):
        j, o = divmod(5 * k, STEP)
        view = views[j, :rows, :]
        return (pltpu.roll(view, LANES - o, 1) if o else view).astype(BF16)

    def halo_windows():
        line = lax.broadcasted_iota(jnp.int32, (16, LANES), 0)
        total = jnp.zeros((16, LANES), F32)
        for k in range(16):
            j, o = divmod(5 * k, STEP)
            block = jnp.broadcast_to(views[j, rows : rows + 1, :], (16, LANES))
            if o:
                block = pltpu.roll(block, LANES - o, 1)
            total = jnp.where(line == k // 2 + 8 * (k % 2), block, total)
        return total.astype(BF16)

    def split(chunk):
        ends = [0, 9, 17, 33, 49, 64]
        return list(range(ends[chunk], ends[chunk + 1]))

    def multiply1(chunk):
        phases = split(chunk)
        acc = acc1[chunk % 3]
        for s in range(0, len(phases), 4):
            group = phases[s : s + 4]
            blocks = [windows(k) for k in group]
            size = len(group) * rows
            if chunk == 0 and s + 4 >= len(phases):
                blocks.append(halo_windows())
                size += 16
            acc[s * rows : s * rows + size, :] = jnp.dot(
                jnp.concatenate(blocks, axis=0), kernel1[...], preferred_element_type=F32
            )

    def finish1(chunk):
        phases = split(chunk)
        acc = acc1[chunk % 3]
        if chunk == 0:
            at = len(phases) * rows
            halo1[0:16, :] = unit_gelu(acc[at : at + 16, :], EPS)
        for index, k in enumerate(phases):
            dest = e1 if k % 2 == 0 else o1
            for r in range(0, rows, 16):
                block = acc[index * rows + r : index * rows + r + 16, :]
                dest[k // 2 * rows + r : k // 2 * rows + r + 16, :] = unit_gelu(block, EPS).astype(BF16)

    def halo_row(halo):
        return jnp.concatenate([halo[c, 0:1, :] for c in range(halo.shape[0])], axis=1)

    def wrap(even, halo, blocks):
        rolled = pltpu.roll(even[:rows, :].astype(F32), rows - 1, 0)
        last = lax.broadcasted_iota(jnp.int32, rolled.shape, 0) == rows - 1
        even[blocks * rows : (blocks + 1) * rows, :] = jnp.where(last, halo, rolled).astype(BF16)

    def halo_taps(halo, interleaved):
        if interleaved:
            pieces = halo.shape[0]
            taps = [
                jnp.concatenate([halo[c, pl.ds(offset, 8, stride=2), :] for c in range(pieces)], axis=1)
                for offset in range(3)
            ]
        else:
            taps = [halo[0:8, :], halo[8:16, :], pltpu.roll(halo[0:8, :], 7, 0)]
        taps = [jnp.concatenate([tap, jnp.zeros_like(tap)], axis=0).astype(BF16) for tap in taps]
        return jnp.concatenate(taps, axis=1)

    def multiply(even, odd, weight, taps, first, phases, acc, halo=None):
        at, size = first * rows, phases * rows
        inputs = [even[at : at + size, :], odd[at : at + size, :]]
        if taps == 3:
            inputs.append(even[at + rows : at + rows + size, :])
        left = jnp.concatenate(inputs, axis=1)
        if halo is not None:
            left = jnp.concatenate([left, halo], axis=0)
        acc[: left.shape[0], :] = jnp.dot(left, weight[...], preferred_element_type=F32)

    def finish(first, phases, acc, dest_even, dest_odd, halo=None):
        if halo is not None:
            at = phases * rows
            ends = norm_unit_gelu(acc[at : at + 16, :], 2.0 * EPS)
            for c in range(halo.shape[0]):
                halo[c, 0:8, :] = ends[:8, c * LANES : (c + 1) * LANES]
        for p in range(phases):
            k = first + p
            dest = dest_even if k % 2 == 0 else dest_odd
            for r in range(0, rows, 16):
                block = acc[p * rows + r : p * rows + r + 16, :]
                dest[k // 2 * rows + r : k // 2 * rows + r + 16, :] = norm_unit_gelu(block, 2.0 * EPS).astype(BF16)

    mids = [mid_ref.at[i] for i in range(4)]
    tails = [tail_ref.at[i] for i in range(2)]
    for halo in (halo2, halo3, halo4):
        halo[...] = jnp.zeros_like(halo)

    layers = {
        2: (e1, o1, e2, o2, mids[0], 3, acc2, halo1, halo2, 16),
        3: (e2, o2, e3, o3, mids[1], 3, acc3, halo2, halo3, 8),
        4: (e3, o3, e4, o4, mids[2], 3, acc4, halo3, halo4, 4),
        5: (e4, o4, e5, o5, mids[3], 3, acc5, None, None, 0),
        6: (e5, o5, e6, o6, tails[0], 2, acc6, None, None, 0),
    }

    def m(layer, first, last, slot):
        even, odd, _, _, weight, taps, acc, halo, _, _ = layers[layer]
        halo = halo_taps(halo, layer > 2) if halo is not None and first == 0 else None
        multiply(even, odd, weight, taps, first, last - first, acc[slot], halo)

    def f(layer, first, last, slot):
        _, _, even, odd, _, _, acc, _, halo, blocks = layers[layer]
        halo = halo if first == 0 else None
        finish(first, last - first, acc[slot], even, odd, halo)
        if halo is not None:
            wrap(even, halo_row(halo), blocks)

    multiply1(0)
    multiply1(1)
    finish1(0)
    m(2, 0, 4, 2)
    multiply1(2)
    finish1(1)
    wrap(e1, halo1[0:1, :], 32)
    m(2, 4, 8, 0)
    f(2, 0, 4, 2)
    finish1(2)
    m(2, 8, 16, 1)
    multiply1(3)
    f(2, 4, 8, 0)
    finish1(3)
    m(2, 16, 24, 2)
    multiply1(4)
    f(2, 8, 16, 1)
    finish1(4)
    m(2, 24, 32, 0)
    f(2, 16, 24, 2)
    m(3, 0, 11, 0)
    f(2, 24, 32, 0)
    m(3, 11, 16, 1)
    f(3, 0, 11, 0)
    m(4, 0, 5, 0)
    f(3, 11, 16, 1)
    m(4, 5, 8, 1)
    f(4, 0, 5, 0)
    m(5, 0, 2, 0)
    f(4, 5, 8, 1)
    m(5, 2, 4, 1)
    f(5, 0, 2, 0)
    m(6, 0, 1, 0)
    f(5, 2, 4, 1)
    m(6, 1, 2, 1)
    f(6, 0, 1, 0)
    f(6, 1, 2, 1)
    multiply(e6, o6, tails[1], 2, 0, 1, acc7)
    for r in range(0, rows, 16):
        out_ref[r : r + 16, :] = (norm_unit_gelu(acc7[r : r + 16, :], 2.0 * EPS) * HALF_ROOT).astype(BF16)


def means(n, reach, feature_ref, length_ref, out_ref, send, recv, send_sem, recv_sem, drain):
    me = lax.axis_index("dp")
    rows, channels = feature_ref.shape
    pieces = channels // LANES
    links = [link for k in range(reach, 0, -1) for link in ((k, k - 1), (-k, reach + k - 1))]

    def inside(k):
        return (me + k < n) & (me + k >= 0)

    base = me.astype(F32) * rows
    _, _, start_col, end_col, _ = spans(rows, rows, length_ref)
    start_row = to_row(start_col)
    end_row = to_row(end_col)
    features = feature_ref[...]
    line = iota((16, rows), 1) + base
    last = line >= start_row[:, rows - 1 : rows]
    initial = line < end_row[:, 0:1]
    pick = jnp.where(iota((16, rows), 0) == 0.0, jnp.where(last, 1.0, 0.0), jnp.where(initial, 1.0, 0.0))
    edges = jnp.dot(pick.astype(BF16), features, preferred_element_type=F32)
    for index in range(2):
        for piece in range(pieces):
            send[index, piece : piece + 1, :] = edges[index : index + 1, piece * LANES : (piece + 1) * LANES]

    def copy(k, slot):
        return pltpu.make_async_remote_copy(
            src_ref=send.at[0 if k > 0 else 1],
            dst_ref=recv.at[slot],
            send_sem=send_sem.at[slot],
            recv_sem=recv_sem.at[slot],
            device_id={"dp": me + k},
        )

    for k, slot in links:
        @pl.when(inside(k))
        def _():
            copy(k, slot).start()
    local = iota((rows, rows), 1) + base
    within = jnp.where((start_col <= local) & (local < end_col), 1.0, 0.0).astype(BF16)
    totals = jnp.dot(within, features, preferred_element_type=F32)
    share = 1.0 / (end_col - start_col)
    from_below = start_col < base
    from_above = end_col > base + rows
    first_start, last_end = start_row[:, 0:1], end_row[:, rows - 1 : rows]
    drain()
    for k, slot in links:
        @pl.when(inside(-k))
        def _():
            copy(-k, slot).wait_recv()
    below = jnp.zeros((8, LANES), F32)
    above = jnp.zeros((8, LANES), F32)
    for k, slot in links:
        if k > 0:
            below = below + jnp.where(first_start <= base - (k - 1) * rows - 1.0, recv[slot], 0.0)
        else:
            above = above + jnp.where(last_end > base - k * rows, recv[slot], 0.0)

    def widen(tile):
        return jnp.concatenate([tile[piece : piece + 1, :] for piece in range(pieces)], axis=1)

    totals = totals + jnp.where(from_below, widen(below), 0.0) + jnp.where(from_above, widen(above), 0.0)
    out_ref[...] = (features.astype(F32) - totals * share).astype(BF16)
    for k, slot in links:
        @pl.when(inside(k))
        def _():
            copy(k, slot).wait_send()


def frontend_kernel(
    n, packing, reach,
    wave_hbm, slot_hbm, length_hbm, trim_hbm, first_hbm, mid_hbm, tail_hbm, out_ref,
    wave, slot, length, trim, first, load_sem, pick, marks,
    send, recv, send_sem, recv_sem, in_sem,
    mid, tail, weight_sem, features, edges, far, edge_send_sem, edge_recv_sem,
    limit, kernel1, views, *work,
):
    small = [
        pltpu.make_async_copy(source, target, load_sem.at[i])
        for i, (source, target) in enumerate(
            ((slot_hbm, slot), (wave_hbm, wave), (length_hbm, length), (trim_hbm, trim), (first_hbm, first))
        )
    ]
    for load in small:
        load.start()
    greet(n)
    loads = [pltpu.make_async_copy(mid_hbm.at[i], mid.at[i], weight_sem.at[i]) for i in range(4)]
    loads.append(pltpu.make_async_copy(tail_hbm, tail, weight_sem.at[4]))
    for load in loads:
        load.start()
    rows = wave.shape[0]
    far[...] = jnp.zeros_like(far)
    edges[...] = jnp.zeros_like(edges)
    enter, begin, finish, drain = exchange(n, packing.stride, send, recv, send_sem, recv_sem, in_sem)
    small[0].wait()
    choose(n, packing, slot, pick, marks)
    enter()
    small[1].wait()
    pack(wave, pick, marks, send)
    begin()
    small[2].wait()
    small[3].wait()
    small[4].wait()
    keep_limit(limit.shape[0], rows, length, trim, limit)
    first_kernel(first, kernel1)
    finish()
    for load in loads:
        load.wait()
    unpack(n, packing, rows, recv, limit, views)
    split = iter(work)
    single = [next(split) for _ in range(16)]
    accs = [[next(split) for _ in range(3)] for _ in range(6)] + list(split)
    convs(rows, views, kernel1, mid, tail, features, single + accs)
    means(n, reach, features, length, out_ref, edges, far, edge_send_sem, edge_recv_sem, drain)


def per_device(wave, row_slot, frame_lengths, sample_trim, first_weight, mid_weight, tail_weight):
    rows = wave.shape[0]
    taps, channels = first_weight.shape
    rolls = frame_lengths.shape[0]
    n = lax.axis_size("dp")
    packing = Packing(rows // n + 2)
    reach = min((MAXLEN + rows - 2) // rows, n - 1)
    mid = mid_weight.reshape(4, 3 * channels, channels)
    tail = tail_weight.reshape(2, 2 * channels, channels)
    vmem = pl.BlockSpec(memory_space=pltpu.VMEM)
    outside = pl.BlockSpec(memory_space=pl.ANY)
    message = (n * packing.stride, LANES)
    frames = rows + 16

    def slab(phases):
        return pltpu.VMEM((phases * rows, channels), BF16)

    halo = pltpu.VMEM((channels // LANES, 24, LANES), F32)

    def total(size):
        return pltpu.VMEM((size, channels), F32)

    return pl.pallas_call(
        functools.partial(frontend_kernel, n, packing, reach),
        out_shape=pltpu.VMEM((rows, channels), BF16),
        in_specs=[outside] * 7,
        out_specs=vmem,
        scratch_shapes=[
            pltpu.VMEM(wave.shape, F32),
            pltpu.VMEM((1, rows), jnp.int32),
            pltpu.VMEM((1, rolls), jnp.int32),
            pltpu.VMEM((1, rolls), jnp.int32),
            pltpu.VMEM((taps, channels), F32),
            pltpu.SemaphoreType.DMA((5,)),
            pltpu.VMEM((message[0], 6 * rows), BF16),
            pltpu.VMEM((rows, LANES), F32),
            pltpu.VMEM(message, F32),
            pltpu.VMEM(message, F32),
            pltpu.SemaphoreType.DMA((n,)),
            pltpu.SemaphoreType.DMA((n,)),
            pltpu.SemaphoreType.REGULAR((n,)),
            pltpu.VMEM(mid.shape, BF16),
            pltpu.VMEM(tail.shape, BF16),
            pltpu.SemaphoreType.DMA((5,)),
            pltpu.VMEM((rows, channels), BF16),
            pltpu.VMEM((2, 8, LANES), F32),
            pltpu.VMEM((2 * reach, 8, LANES), F32),
            pltpu.SemaphoreType.DMA((2 * reach,)),
            pltpu.SemaphoreType.DMA((2 * reach,)),
            pltpu.VMEM((frames, LANES), F32),
            pltpu.VMEM((LANES, channels), BF16),
            pltpu.VMEM((BLOCK // STEP, frames, LANES), F32),
            slab(33), slab(32), slab(17), slab(16), slab(9), slab(8), slab(5), slab(4),
            slab(2), slab(2), slab(1), slab(1),
            total(16), halo, halo, halo,
            *[total(17 * rows + 16)] * 3, *[total(9 * rows + 16)] * 3, *[total(11 * rows + 16)] * 3,
            *[total(5 * rows + 16)] * 3, *[total(4 * rows)] * 3, *[total(2 * rows)] * 3, total(rows),
        ],
        compiler_params=pltpu.CompilerParams(
            collective_id=0, has_side_effects=True, vmem_limit_bytes=48 * 1024 * 1024
        ),
        name="frontend",
    )(*[pltpu.with_memory_space_constraint(x, pltpu.HBM) for x in (
        wave, row_slot.reshape(1, -1), frame_lengths.reshape(1, -1), sample_trim.reshape(1, -1),
        first_weight, mid, tail)]
    )


def solution(mesh):
    placed = (
        P(("groups", "dp"), None),
        P(("groups", "dp")),
        P("groups"),
        P("groups"),
        P(),
        P(),
        P(),
    )
    return jax.shard_map(
        per_device, mesh=mesh, in_specs=placed, out_specs=P(("groups", "dp"), None), check_vma=False
    )
```
